768 devices in a mesh: blk: 24 (over z_lo, x), uly: 32 (over z_hi, y, core).
Axes of the slice: x: 4, y: 8, z: 12 (z_hi: 2, z_lo: 6; z = z_hi * 6 + z_lo), core: 2. Of those that a mesh axis runs over, the one named last changes fastest.
Arguments:
- queries: bfloat16 [98304, 4096], P(('blk', 'uly')), may hold values from -1.5 to 1.5
- keys: bfloat16 [98304, 1024], P(('blk', 'uly')), may hold values from -1.5 to 1.5
- values: bfloat16 [98304, 1024], P(('blk', 'uly')), may hold values from -6 to 6
- grad_out: bfloat16 [98304, 4096], P(('blk', 'uly')), may hold values from -96 to 96
- row_lse: float32 [98304, 32], P('blk', 'uly'), may hold values from 6 to 7.5
- row_delta: float32 [98304, 32], P('blk', 'uly'), may hold values from -960 to 960
- pattern: int32 [768, 2], replicated, may hold values from 0 to 767, as said below
- memory_keys: bfloat16 [128, 4096], P(None, 'uly'), may hold values from -1.5 to 1.5
- memory_values: bfloat16 [128, 4096], P(None, 'uly'), may hold values from -6 to 6
Outputs:
- grad_queries: bfloat16 [98304, 4096], P(('blk', 'uly'))
- grad_keys: float32 [98304, 1024], P(('blk', 'uly'))
- grad_values: float32 [98304, 1024], P(('blk', 'uly'))
- grad_memory_keys: float32 [128, 4096], P(None, 'uly')
- grad_memory_values: float32 [128, 4096], P(None, 'uly')
The draws below stay inside these ranges and needn't reach their ends.
Inputs may be any that keep to these rules, and one draw needn't show every extreme that they name: `pattern`: query block b lies in span b // 32. The rows of one span name exactly one block of every span that is neither that span nor beside it; all their other named blocks lie in the span itself.
All inputs are finite; a program needn't handle non-finite values.
Results may differ from the reference program's by a relative error of at most 0.0085.
Values may be sent and summed in bfloat16 or wider, within the bound.
A program may use at most 64 MiB of HBM per device.

```python
import jax
import jax.numpy as jnp
from jax import lax

QUERY_HEADS = 32
KEY_HEADS = 8
HEAD_FEATURES = 128
BLOCK = 128
RANDOM = 2
QUERY_PER_KEY = 4
QB_DEV = 32
SPANS = 24
SEQUENCE_TOKENS = 98304
NBLOCKS = 768


def draw_pattern(key, part):
    entries = QB_DEV * RANDOM

    def for_span(span_id, span_key):
        key_a, key_b = jax.random.split(span_key, 2)
        entry_ids = jnp.arange(entries, dtype=jnp.int32)
        left_count = jnp.maximum(span_id - 1, 0)
        far_count = SPANS - 1 - (span_id > 0).astype(jnp.int32) - (span_id < SPANS - 1).astype(jnp.int32)
        far_owner = jnp.where(entry_ids < left_count, entry_ids, entry_ids - left_count + span_id + 2)
        owners = jnp.where(entry_ids < far_count, far_owner, span_id)
        blocks = jax.random.randint(key_a, (entries,), 0, QB_DEV)
        picked = owners * QB_DEV + blocks
        shuffled = jax.random.permutation(key_b, entries)
        return picked[shuffled].reshape(QB_DEV, RANDOM)
    span_ids = jnp.arange(SPANS, dtype=jnp.int32)
    span_keys = jax.random.split(key, SPANS)
    all_rows = jax.vmap(for_span)(span_ids, span_keys)
    return all_rows.reshape(NBLOCKS, RANDOM).astype(jnp.int32)


def block_scale(stream_key, extent, cuts, least, high):
    level = 1.0
    for axis_at, shards_of in cuts:
        draws = jax.random.uniform(jax.random.fold_in(jax.random.fold_in(stream_key, 6), axis_at), (shards_of,), jnp.float32, least / len(cuts), high / len(cuts))
        level = level * jnp.repeat(jnp.exp(draws), extent[axis_at] // shards_of).reshape((-1,) + (1,) * (len(extent) - 1 - axis_at))
    return level


def gaussian(stream_key, dims, deviation, limit, pieces=(), kind=jnp.bfloat16):
    drawn = deviation * jax.random.normal(stream_key, dims, jnp.float32)
    if pieces:
        drawn = drawn * block_scale(stream_key, dims, pieces, -0.22, 0.18)
    return jnp.clip(drawn, -limit, limit).astype(kind)


def setup_inputs(seed: int = 0) -> dict:
    key_of = jax.random.split(jax.random.key(seed), 10)
    queries = jnp.clip(jax.random.uniform(key_of[0], (SEQUENCE_TOKENS, QUERY_HEADS * HEAD_FEATURES), jnp.float32, -1.5, 1.5) * block_scale(key_of[0], (SEQUENCE_TOKENS, QUERY_HEADS * HEAD_FEATURES), ((0, 768),), -0.4, 0.0), -1.5, 1.5).astype(jnp.bfloat16)
    keys = jnp.clip(jax.random.uniform(key_of[1], (SEQUENCE_TOKENS, KEY_HEADS * HEAD_FEATURES), jnp.float32, -1.5, 1.5) * block_scale(key_of[1], (SEQUENCE_TOKENS, KEY_HEADS * HEAD_FEATURES), ((0, 768),), -0.4, 0.0), -1.5, 1.5).astype(jnp.bfloat16)
    values = gaussian(key_of[2], (SEQUENCE_TOKENS, KEY_HEADS * HEAD_FEATURES), 1.0, 6.0, ((0, 768),))
    grad_out = gaussian(key_of[3], (SEQUENCE_TOKENS, QUERY_HEADS * HEAD_FEATURES), 16.0, 96.0, ((0, 768),))
    row_lse = jnp.clip(6.0 + 1.5 * jax.random.uniform(key_of[4], (SEQUENCE_TOKENS, QUERY_HEADS), jnp.float32) ** block_scale(key_of[4], (SEQUENCE_TOKENS, QUERY_HEADS), ((0, 24), (1, 32)), -0.2, 0.2), 6.0, 7.5)
    row_delta = gaussian(key_of[5], (SEQUENCE_TOKENS, QUERY_HEADS), 160.0, 960.0, ((0, 24), (1, 32)), jnp.float32)
    pattern = draw_pattern(jax.random.fold_in(key_of[9], 71), 0)
    memory_keys = jnp.clip(jax.random.uniform(key_of[7], (BLOCK, QUERY_HEADS * HEAD_FEATURES), jnp.float32, -1.5, 1.5) * block_scale(key_of[7], (BLOCK, QUERY_HEADS * HEAD_FEATURES), ((1, 32),), -0.4, 0.0), -1.5, 1.5).astype(jnp.bfloat16)
    memory_values = gaussian(key_of[8], (BLOCK, QUERY_HEADS * HEAD_FEATURES), 1.0, 6.0, ((1, 32),))
    return dict(queries=queries, keys=keys, values=values, grad_out=grad_out, row_lse=row_lse, row_delta=row_delta, pattern=pattern, memory_keys=memory_keys, memory_values=memory_values)


def reference(queries, keys, values, grad_out, row_lse, row_delta, pattern, memory_keys, memory_values):
    score_scale = HEAD_FEATURES ** -0.5
    block_count = SEQUENCE_TOKENS // BLOCK
    block_ids = jnp.arange(block_count, dtype=jnp.int32)
    window = jnp.stack([block_ids - 1, block_ids, block_ids + 1], axis=1)
    window_ok = (window >= 0) & (window < block_count)
    key_index = jnp.concatenate([jnp.clip(window, 0, block_count - 1), pattern.astype(jnp.int32)], axis=1)
    pair_ok = jnp.concatenate([window_ok, jnp.ones((block_count, RANDOM + 1), dtype=bool)], axis=1).astype(jnp.float32)
    seq_terms = RANDOM + 3

    def columns(matrix, column_id):
        return lax.dynamic_slice_in_dim(matrix, column_id * HEAD_FEATURES, HEAD_FEATURES, 1).astype(jnp.float32)

    def per_head(head_id):
        group_id = head_id // QUERY_PER_KEY
        query_blk = columns(queries, head_id).reshape(block_count, BLOCK, HEAD_FEATURES)
        dout_blk = columns(grad_out, head_id).reshape(block_count, BLOCK, HEAD_FEATURES)
        key_rows = columns(keys, group_id).reshape(block_count, BLOCK, HEAD_FEATURES)
        value_rows = columns(values, group_id).reshape(block_count, BLOCK, HEAD_FEATURES)
        mem_key = columns(memory_keys, head_id)
        mem_value = columns(memory_values, head_id)
        key_sets = jnp.concatenate([key_rows[key_index], jnp.broadcast_to(mem_key, (block_count, 1, BLOCK, HEAD_FEATURES))], axis=1)
        value_sets = jnp.concatenate([value_rows[key_index], jnp.broadcast_to(mem_value, (block_count, 1, BLOCK, HEAD_FEATURES))], axis=1)
        lse_blk = lax.dynamic_slice_in_dim(row_lse, head_id, 1, 1).reshape(block_count, BLOCK)
        delta_blk = lax.dynamic_slice_in_dim(row_delta, head_id, 1, 1).reshape(block_count, BLOCK)
        scores = jnp.einsum('nad,nskd->nsak', query_blk, key_sets) * score_scale
        weights = jnp.exp(scores - lse_blk[:, None, :, None]) * pair_ok[:, :, None, None]
        dweights = jnp.einsum('nad,nskd->nsak', dout_blk, value_sets)
        dscores = weights * (dweights - delta_blk[:, None, :, None])
        weight_bf = lax.optimization_barrier(weights.astype(jnp.bfloat16)).astype(jnp.float32)
        dscore_bf = lax.optimization_barrier(dscores.astype(jnp.bfloat16)).astype(jnp.float32)
        grad_q = (jnp.einsum('nsak,nskd->nad', dscore_bf, key_sets) * score_scale).astype(jnp.bfloat16)
        key_term = jnp.einsum('nsak,nad->nskd', dscore_bf, query_blk) * score_scale
        key_term = lax.optimization_barrier(key_term.astype(jnp.bfloat16)).astype(jnp.float32)
        value_term = jnp.einsum('nsak,nad->nskd', weight_bf, dout_blk)
        value_term = lax.optimization_barrier(value_term.astype(jnp.bfloat16)).astype(jnp.float32)
        head_dk = jnp.zeros((block_count, BLOCK, HEAD_FEATURES), jnp.float32).at[key_index].add(key_term[:, :seq_terms])
        head_dv = jnp.zeros((block_count, BLOCK, HEAD_FEATURES), jnp.float32).at[key_index].add(value_term[:, :seq_terms])
        mem_dk = jnp.sum(key_term[:, seq_terms], axis=0)
        mem_dv = jnp.sum(value_term[:, seq_terms], axis=0)
        return (grad_q.reshape(SEQUENCE_TOKENS, HEAD_FEATURES), head_dk.astype(jnp.bfloat16).reshape(SEQUENCE_TOKENS, HEAD_FEATURES),
                head_dv.astype(jnp.bfloat16).reshape(SEQUENCE_TOKENS, HEAD_FEATURES), mem_dk, mem_dv)

    results = lax.map(per_head, jnp.arange(QUERY_HEADS, dtype=jnp.int32))
    grad_q_all, dk_heads, dv_heads, mk_heads, mv_heads = results
    grad_queries = grad_q_all.transpose(1, 0, 2).reshape(SEQUENCE_TOKENS, QUERY_HEADS * HEAD_FEATURES)

    def group_sum(stacked_parts, count_of_rows):
        summed_terms = jnp.sum(stacked_parts.astype(jnp.float32).reshape(KEY_HEADS, QUERY_PER_KEY, count_of_rows, HEAD_FEATURES), axis=1)
        return summed_terms.transpose(1, 0, 2).reshape(count_of_rows, KEY_HEADS * HEAD_FEATURES)

    def rows_by_head(stacked_parts):
        return stacked_parts.transpose(1, 0, 2).reshape(BLOCK, QUERY_HEADS * HEAD_FEATURES)

    return (grad_queries, group_sum(dk_heads, SEQUENCE_TOKENS), group_sum(dv_heads, SEQUENCE_TOKENS),
            rows_by_head(mk_heads), rows_by_head(mv_heads))
```

```python
import functools

import jax
import jax.numpy as jnp
from jax import lax
from jax.experimental import pallas as pl
from jax.experimental.pallas import tpu as pltpu
from jax.sharding import PartitionSpec as P

QUERY_HEADS = 32
KEY_HEADS = 8
FEATURES = 128
BLOCK = 128
RANDOM = 2
SLOTS = 3 + RANDOM
SCALE = FEATURES ** (-0.5)
MESH = pl.DeviceIdType.MESH

SPANS, PLACES = 24, 32
HALF = PLACES // 2
YS = HALF // 2
X, Z = 4, 6
PARTS = 8
ROWS = 4 * BLOCK // PARTS

F32, BF16 = jnp.float32, jnp.bfloat16


def position():
    s, u = lax.axis_index("blk"), lax.axis_index("uly")
    return s, u, u // HALF, u % HALF, u % 2


def far_place(s, u, t):
    a, b = s // X, t // X
    d = (b - a + Z) % Z
    even = (s % X + t % X) % 2 == 0
    three = jnp.where((a < Z // 2) == even, Z // 2, -(Z // 2))
    step = jnp.where(d == Z // 2, three, jnp.where(d < Z // 2, d, d - Z))
    z = ((u // HALF) * Z + a + step + 2 * Z) % (2 * Z)
    return (z // Z) * HALF + u % HALF


def remote(src, dst, sent, got, blk, uly):
    return pltpu.make_async_remote_copy(
        src_ref=src, dst_ref=dst, send_sem=sent, recv_sem=got, device_id=(blk, uly), device_id_type=MESH
    )


def send(src, dst, sent, got, blk, uly, here):
    @pl.when(jnp.logical_not(here))
    def _():
        remote(src, dst, sent, got, blk, uly).start()

    @pl.when(here)
    def _():
        pltpu.make_async_copy(src, dst, got).start()


def wait(ref, sem):
    pltpu.make_async_copy(ref, ref, sem).wait()


def loop(n, body):
    def step(i, carry):
        body(i)
        return carry

    lax.fori_loop(0, n, step, 0)


def greet(blk, uly):
    pl.semaphore_signal(pltpu.get_barrier_semaphore(), inc=1, device_id=(blk, uly), device_id_type=MESH)


def others(n, me, body):
    def step(i):
        @pl.when(i != me)
        def _():
            body(i)

    loop(n, step)


def gather(
    send_ref, q_ref, do_ref, k_ref, v_ref, stat_ref, mem_ref,
    qh_ref, doh_ref, own_ref, other_ref, far_ref, far_other_ref, stat_out, mem_out,
    out_ref, s_kv, r_kv, s_q, r_q, s_do, r_do, s_z, r_z, s_core, r_core, s_far, r_far, s_stat, r_stat, s_mem, r_mem,
):
    s, u, half, p_me, core = position()
    others(PLACES, u, lambda p: greet(s, p))
    others(SPANS, s, lambda t: greet(t, far_place(s, u, t)))
    pl.semaphore_wait(pltpu.get_barrier_semaphore(), PLACES - 1 + SPANS - 1)

    def columns(ref, i, width):
        return ref.at[:, pl.ds(pl.multiple_of(i * width, width), width)]

    first = half * HALF

    def kv_to(y):
        for kind, ref in ((0, k_ref), (1, v_ref)):
            place = first + 2 * y + kind
            send(columns(ref, y, FEATURES), own_ref.at[first + p_me], s_kv, r_kv, s, place, place == u)

    loop(YS, kv_to)
    for z in range(2):
        place = z * HALF + u // 2
        send(stat_ref.at[z], stat_out.at[u % 2], s_stat.at[z], r_stat, s, place, place == u)
        send(mem_ref, mem_out.at[u % 2], s_mem.at[z], r_mem, s, place, place == u)

    mine = own_ref.at[pl.ds(first, HALF)]
    wait(mine, r_kv)
    swap = remote(mine, mine, s_z, r_z, s, (u + HALF) % PLACES)
    swap.start()
    core_peer = u + 1 - 2 * core
    onward = remote(mine, other_ref.at[pl.ds(first, HALF)], s_core.at[0], r_core.at[0], s, core_peer)
    onward.start()

    def q_to(p):
        here = p == p_me
        send(columns(q_ref, p, 2 * FEATURES), qh_ref.at[p_me], s_q, r_q, s, first + p, here)
        send(columns(do_ref, p, 2 * FEATURES), doh_ref.at[p_me], s_do, r_do, s, first + p, here)

    loop(HALF, q_to)
    second = HALF - first
    theirs = own_ref.at[pl.ds(second, HALF)]
    wait(theirs, r_z)
    onward2 = remote(theirs, other_ref.at[pl.ds(second, HALF)], s_core.at[1], r_core.at[1], s, core_peer)
    onward2.start()

    def far_to(t):
        out_ref[t] = own_ref[send_ref[t]]
        remote(out_ref.at[t], far_ref.at[s], s_far, r_far, t, far_place(s, u, t)).start()

    others(SPANS, s, far_to)
    wait(far_ref.at[pl.ds(0, SPANS - 1)], r_far)
    onward3 = remote(far_ref, far_other_ref, s_core.at[2], r_core.at[2], s, core_peer)
    onward3.start()
    wait(qh_ref, r_q)
    wait(doh_ref, r_do)
    wait(stat_out, r_stat)
    wait(mem_out, r_mem)
    onward.wait_recv()
    onward2.wait_recv()
    onward3.wait_recv()
    wait(own_ref.at[pl.ds(0, HALF - 1)], s_kv)
    wait(qh_ref.at[pl.ds(0, HALF - 1)], s_q)
    wait(doh_ref.at[pl.ds(0, HALF - 1)], s_do)
    wait(out_ref.at[pl.ds(0, SPANS - 1)], s_far)
    swap.wait_send()
    onward.wait_send()
    onward2.wait_send()
    onward3.wait_send()
    for z in range(2):
        @pl.when(z * HALF + u // 2 != u)
        def _():
            wait(stat_out.at[0], s_stat.at[z])
            wait(mem_out.at[0], s_mem.at[z])


def vmem(n):
    return [pl.BlockSpec(memory_space=pltpu.VMEM)] * n


def hbm(n):
    return [pl.BlockSpec(memory_space=pl.ANY)] * n


SMEM = pl.BlockSpec(memory_space=pltpu.SMEM)
DMA = pltpu.SemaphoreType.DMA


def shape(*dims, dtype=BF16):
    return jax.ShapeDtypeStruct(dims, dtype)


def gather_call(sends, q, do, k, v, stats, mem):
    tile = (BLOCK, FEATURES)
    return pl.pallas_call(
        gather,
        in_specs=[SMEM] + hbm(6),
        out_specs=vmem(8),
        out_shape=[
            shape(HALF, BLOCK, 2 * FEATURES), shape(HALF, BLOCK, 2 * FEATURES),
            shape(PLACES, *tile), shape(PLACES, *tile), shape(SPANS, *tile), shape(SPANS, *tile),
            shape(2, 2, HALF, BLOCK, dtype=F32), shape(2, 2, *tile),
        ],
        scratch_shapes=[pltpu.VMEM((SPANS,) + tile, BF16)]
        + [DMA] * 8
        + [DMA((3,)), DMA((3,)), DMA, DMA, DMA((2,)), DMA, DMA((2,)), DMA],
        compiler_params=pltpu.CompilerParams(collective_id=0, has_side_effects=True),
        name="gather",
    )(sends, q, do, k, v, stats, mem)


def attend(
    meta_ref, idx_ref, q_ref, do_ref, stat_ref, own_ref, other_ref, far_ref, far_other_ref, mem_ref,
    gq_ref, keep_ref, give_ref, dmem_ref, pool_ref, acc_ref, macc_ref,
):
    step = pl.program_id(0)
    steps = pl.num_programs(0)
    core = meta_ref[0]

    @pl.when(step == 0)
    def _():
        acc_ref[...] = jnp.zeros_like(acc_ref)
        macc_ref[...] = jnp.zeros_like(macc_ref)

        @pl.loop(0, PLACES)
        def _(n):
            pool_ref[core, n] = own_ref[n]
            pool_ref[1 - core, n] = other_ref[n]

        @pl.loop(0, SPANS)
        def _(n):
            pool_ref[core, PLACES + n] = far_ref[n]
            pool_ref[1 - core, PLACES + n] = far_other_ref[n]

    def dot(a, b, i, j):
        return lax.dot_general(a, b, (((i,), (j,)), ((), ())), preferred_element_type=F32)

    q = [q_ref[0, :, FEATURES * i : FEATURES * (i + 1)] for i in range(2)]
    do = [do_ref[0, :, FEATURES * i : FEATURES * (i + 1)] for i in range(2)]
    q2 = jnp.concatenate(q, axis=0)
    do2 = jnp.concatenate(do, axis=0)
    lse, delta = [
        jnp.concatenate([stat_ref[i, kind, pl.ds(step, 1), :] for i in range(2)], axis=1) for kind in range(2)
    ]
    which = [idx_ref[step, j] for j in range(SLOTS)]
    keys = jnp.concatenate([pool_ref[0, w] for w in which], axis=0)
    values = jnp.concatenate([pool_ref[1, w] for w in which], axis=0)

    weights = jnp.exp(dot(keys, q2, 1, 1) * SCALE - lse)
    dscores = weights * (dot(values, do2, 1, 1) - delta)
    row = lax.broadcasted_iota(jnp.int32, (SLOTS * BLOCK, 1), 0)
    left, right = idx_ref[step, SLOTS], idx_ref[step, SLOTS + 1]
    keep = ((row >= BLOCK) | (left > 0)) & ((row < 2 * BLOCK) | (row >= 3 * BLOCK) | (right > 0))
    weight_bf = jnp.where(keep, weights, 0.0).astype(BF16)
    dscore_bf = jnp.where(keep, dscores, 0.0).astype(BF16)
    dkey = dot(dscore_bf, q2, 1, 0)
    dvalue = dot(weight_bf, do2, 1, 0)
    dquery = dot(dscore_bf, keys, 0, 0)
    for j in range(SLOTS):
        rows = slice(BLOCK * j, BLOCK * (j + 1))
        acc_ref[0, which[j]] += dkey[rows]
        acc_ref[1, which[j]] += dvalue[rows]

    for i in range(2):
        cols = slice(FEATURES * i, FEATURES * (i + 1))
        w = jnp.exp(dot(mem_ref[i, 0], q[i], 1, 1) * SCALE - lse[:, cols])
        ds = (w * (dot(mem_ref[i, 1], do[i], 1, 1) - delta[:, cols])).astype(BF16)
        macc_ref[i, 0] += dot(ds, q[i], 1, 0)
        macc_ref[i, 1] += dot(w.astype(BF16), do[i], 1, 0)
        gq = dquery[BLOCK * i : BLOCK * (i + 1)] + dot(ds, mem_ref[i, 0], 0, 0)
        gq_ref[0, :, cols] = (gq * SCALE).astype(BF16)

    @pl.when(step == steps - 1)
    def _():
        mine = jnp.where(core == 0, SCALE, 1.0)
        theirs = jnp.where(core == 0, 1.0, SCALE)

        @pl.loop(0, PLACES + SPANS)
        def _(n):
            keep_ref[n] = (acc_ref[core, n] * mine).astype(BF16)
            give_ref[n] = (acc_ref[1 - core, n] * theirs).astype(BF16)

        for i in range(2):
            dmem_ref[i, 0] = macc_ref[i, 0] * SCALE
            dmem_ref[i, 1] = macc_ref[i, 1]


def attend_call(meta, idx, q, do, stats, own, other, far, far_other, mem):
    tile = (BLOCK, FEATURES)
    pool = PLACES + SPANS

    def per_block():
        return pl.BlockSpec((1, BLOCK, 2 * FEATURES), lambda b, *_: (b, 0, 0))

    def whole(dims):
        return pl.BlockSpec(dims, lambda b, *_: (0,) * len(dims))

    return pl.pallas_call(
        attend,
        grid_spec=pltpu.PrefetchScalarGridSpec(
            num_scalar_prefetch=2,
            grid=(HALF,),
            in_specs=[per_block(), per_block()] + [whole(a.shape) for a in (stats, own, other, far, far_other, mem)],
            out_specs=[per_block(), whole((pool,) + tile), whole((pool,) + tile), whole((2, 2) + tile)],
            scratch_shapes=[
                pltpu.VMEM((2, pool) + tile, BF16),
                pltpu.VMEM((2, pool) + tile, F32),
                pltpu.VMEM((2, 2) + tile, F32),
            ],
        ),
        out_shape=[
            shape(HALF, BLOCK, 2 * FEATURES), shape(pool, *tile), shape(pool, *tile), shape(2, 2, *tile, dtype=F32),
        ],
        name="attend",
    )(meta, idx, q, do, stats, own, other, far, far_other, mem)


def part_peer(s, r):
    return ((s // X) // 2 * 2 + r % 2) * X + r // 2


def my_part(s):
    return s % X * 2 + s // X % 2


def give_back(
    keep_ref, give_ref, dmem_ref, total_ref, back_ref, part_ref,
    got_ref, out_ref, parts_ref, s_core, r_core, s_far, r_far, s_part, r_part,
):
    s, u, half, p_me, core = position()
    core_peer = u + 1 - 2 * core
    r_me = my_part(s)
    greet(s, core_peer)
    others(SPANS, s, lambda t: greet(t, far_place(s, u, t)))
    others(PARTS, r_me, lambda r: greet(part_peer(s, r), u))
    pl.semaphore_wait(pltpu.get_barrier_semaphore(), 1 + SPANS - 1 + PARTS - 1)

    far, near = pl.ds(PLACES, SPANS), pl.ds(0, PLACES)
    swap_far = remote(give_ref.at[far], got_ref.at[far], s_core.at[0], r_core.at[0], s, core_peer)
    swap_far.start()
    swap_near = remote(give_ref.at[near], got_ref.at[near], s_core.at[1], r_core.at[1], s, core_peer)
    swap_near.start()

    def part_to(r):
        remote(dmem_ref.at[r], parts_ref.at[r_me], s_part, r_part, part_peer(s, r), u).start()

    others(PARTS, r_me, part_to)
    swap_far.wait_recv()

    def far_to(t):
        out_ref[t] = (keep_ref[PLACES + t].astype(F32) + got_ref[PLACES + t].astype(F32)).astype(BF16)
        remote(out_ref.at[t], back_ref.at[s], s_far, r_far, t, far_place(s, u, t)).start()

    others(SPANS, s, far_to)
    swap_near.wait_recv()

    def add(n):
        total_ref[n] = keep_ref[n].astype(F32) + got_ref[n].astype(F32)

    loop(PLACES, add)
    wait(parts_ref.at[pl.ds(0, PARTS - 1)], r_part)
    parts_ref[r_me] = dmem_ref[r_me]
    part_ref[...] = jnp.sum(parts_ref[...], axis=0)
    wait(back_ref.at[pl.ds(0, SPANS - 1)], r_far)
    wait(out_ref.at[pl.ds(0, SPANS - 1)], s_far)
    wait(parts_ref.at[pl.ds(0, PARTS - 1)], s_part)
    swap_far.wait_send()
    swap_near.wait_send()


def give_back_call(keep, give, dmem):
    tile = (BLOCK, FEATURES)
    return pl.pallas_call(
        give_back,
        in_specs=vmem(3),
        out_specs=vmem(3),
        out_shape=[shape(PLACES, *tile, dtype=F32), shape(SPANS, *tile), shape(ROWS, FEATURES, dtype=F32)],
        scratch_shapes=[
            pltpu.VMEM((PLACES + SPANS,) + tile, BF16),
            pltpu.VMEM((SPANS,) + tile, BF16),
            pltpu.VMEM((PARTS, ROWS, FEATURES), F32),
            DMA((2,)), DMA((2,)), DMA, DMA, DMA, DMA,
        ],
        compiler_params=pltpu.CompilerParams(collective_id=1, has_side_effects=True),
        name="give_back",
    )(keep, give, dmem)


def settle(meta_ref, send_ref, total_ref, back_ref, here_ref, away_ref, acc_ref):
    acc_ref[...] = total_ref[...]
    s, half = meta_ref[1], meta_ref[2]

    @pl.loop(0, SPANS)
    def _(t):
        @pl.when(t != s)
        def _():
            acc_ref[send_ref[t]] += back_ref[t].astype(F32)

    @pl.loop(0, HALF)
    def _(n):
        here_ref[n] = acc_ref[half * HALF + n]
        away_ref[n] = acc_ref[(1 - half) * HALF + n].astype(BF16)


def settle_call(meta, sends, total, back):
    tile = (BLOCK, FEATURES)
    return pl.pallas_call(
        settle,
        in_specs=[SMEM, SMEM] + vmem(2),
        out_specs=vmem(2),
        out_shape=[shape(HALF, *tile, dtype=F32), shape(HALF, *tile)],
        scratch_shapes=[pltpu.VMEM((PLACES,) + tile, F32)],
        name="settle",
    )(meta, sends, total, back)


CHUNKS = 4
RINGS = 6


def deliver(
    gq_ref, here_ref, away_ref, part_ref, gq_out, dk_ref, dv_ref, mem_out,
    got_ref, out_ref, rows_ref, parts_ref, sum_ref,
    s_z, r_z, s_q, r_q, s_rows, r_rows, s_part, r_part, s_mem, r_mem,
):
    s, u, half, p_me, core = position()
    first = half * HALF
    r_me = my_part(s)
    ring_me = (s // X) // 2 * 2 + half
    y = p_me // 2
    head = 4 * y + 2 * core + r_me // 4
    source = first + u // 2

    def ring_peer(r):
        return ((r // 2) * 2 + s // X % 2) * X + s % X, r % 2 * HALF + p_me

    gives = half == y // 4

    def takers(body):
        def step(r):
            blk = part_peer(s, r)

            @pl.when(jnp.logical_not((blk == s) & (head == u)))
            def _():
                body(r, blk)

        loop(PARTS, step)

    def givers(body):
        def step(n):
            blk = part_peer(s, u % 2 * 4 + n)

            @pl.when(jnp.logical_not((blk == s) & (source == u)))
            def _():
                body(blk)

        loop(4, step)

    others(PLACES, u, lambda p: greet(s, p))
    others(RINGS, ring_me, lambda r: greet(*ring_peer(r)))

    @pl.when(gives)
    def _():
        takers(lambda r, blk: greet(blk, head))

    givers(lambda blk: greet(blk, source))
    own = ((r_me // 4 == u % 2) & (source == u)).astype(jnp.int32)
    count = PLACES - 1 + RINGS - 1 + 4 - own + jnp.where(gives, PARTS - own, 0)
    pl.semaphore_wait(pltpu.get_barrier_semaphore(), count)

    each = HALF // CHUNKS
    swaps = []
    for n in range(CHUNKS):
        rows = pl.ds(n * each, each)
        swaps.append(remote(away_ref.at[rows], got_ref.at[rows], s_z.at[n], r_z.at[n], s, (u + HALF) % PLACES))
        swaps[-1].start()

    def part_to(r):
        remote(part_ref, parts_ref.at[ring_me], s_part, r_part, *ring_peer(r)).start()

    others(RINGS, ring_me, part_to)

    def columns(ref, i, width):
        return ref.at[:, pl.ds(pl.multiple_of(i * width, width), width)]

    def gq_to(p):
        send(gq_ref.at[p], columns(gq_out, p_me, 2 * FEATURES), s_q, r_q, s, first + p, p == p_me)

    loop(HALF, gq_to)
    wait(parts_ref.at[pl.ds(0, RINGS - 1)], r_part)
    parts_ref[ring_me] = part_ref[...]
    sum_ref[...] = jnp.sum(parts_ref[...], axis=0)

    def mem_to(r):
        blk = part_peer(s, r)
        send(sum_ref, mem_out.at[r_me % 4], s_mem.at[r], r_mem, blk, head, (blk == s) & (head == u))

    @pl.when(gives)
    def _():
        loop(PARTS, mem_to)

    for n in range(CHUNKS):
        swaps[n].wait_recv()

        def rows_to(i):
            p = n * each + i
            out_ref[p] = (here_ref[p] + got_ref[p].astype(F32)).astype(BF16)
            send(out_ref.at[p], rows_ref.at[p_me], s_rows, r_rows, s, first + p, p == p_me)

        loop(each, rows_to)
    wait(rows_ref, r_rows)
    for head_id in range(KEY_HEADS):
        cols = slice(FEATURES * head_id, FEATURES * (head_id + 1))
        dk_ref[:, cols] = rows_ref[2 * head_id].astype(F32)
        dv_ref[:, cols] = rows_ref[2 * head_id + 1].astype(F32)
    wait(mem_out, r_mem)
    wait(gq_out, r_q)
    wait(out_ref.at[pl.ds(0, HALF - 1)], s_rows)
    wait(gq_out.at[:, pl.ds(0, (HALF - 1) * 2 * FEATURES)], s_q)
    wait(parts_ref.at[pl.ds(0, RINGS - 1)], s_part)
    for n in range(CHUNKS):
        swaps[n].wait_send()

    @pl.when(gives)
    def _():
        takers(lambda r, blk: wait(sum_ref, s_mem.at[r]))


def deliver_call(gq, here, away, part):
    tile = (BLOCK, FEATURES)
    return pl.pallas_call(
        deliver,
        in_specs=vmem(4),
        out_specs=vmem(4),
        out_shape=[
            shape(BLOCK, QUERY_HEADS * FEATURES),
            shape(BLOCK, KEY_HEADS * FEATURES, dtype=F32), shape(BLOCK, KEY_HEADS * FEATURES, dtype=F32),
            shape(4, ROWS, FEATURES, dtype=F32),
        ],
        scratch_shapes=[
            pltpu.VMEM((HALF,) + tile, BF16), pltpu.VMEM((HALF,) + tile, BF16), pltpu.VMEM((HALF,) + tile, BF16),
            pltpu.VMEM((RINGS, ROWS, FEATURES), F32), pltpu.VMEM((ROWS, FEATURES), F32),
            DMA((CHUNKS,)), DMA((CHUNKS,)), DMA, DMA, DMA, DMA, DMA, DMA, DMA((PARTS,)), DMA,
        ],
        compiler_params=pltpu.CompilerParams(collective_id=2, has_side_effects=True),
        name="deliver",
    )(gq, here, away, part)


def shards(queries, keys, values, grad_out, row_lse, row_delta, pattern, memory_keys, memory_values):
    span, place = lax.axis_index("blk"), lax.axis_index("uly")
    half, core = place // HALF, place % 2
    flat = pattern.reshape(SPANS, PLACES * RANDOM)
    ids = jnp.arange(SPANS, dtype=jnp.int32)
    from_me = (flat // PLACES == span) & (ids != span)[:, None]
    named = jnp.sum(jnp.where(from_me, flat % PLACES, 0), axis=1)
    edge = jnp.where(ids > span, PLACES - 1, 0)
    sends = jnp.where(jnp.abs(ids - span) == 1, edge, named)
    mine = lax.dynamic_slice(pattern, (span * PLACES + half * HALF, 0), (HALF, RANDOM))
    mine = jnp.where(mine // PLACES == span, mine % PLACES, PLACES + mine // PLACES)
    b = half * HALF + jnp.arange(HALF, dtype=jnp.int32)
    left_ok = (b > 0) | (span > 0)
    right_ok = (b < PLACES - 1) | (span < SPANS - 1)
    left = jnp.where(b > 0, b - 1, jnp.where(left_ok, PLACES + span - 1, b))
    right = jnp.where(b < PLACES - 1, b + 1, jnp.where(right_ok, PLACES + span + 1, b))
    ends = jnp.stack([left_ok, right_ok], axis=1).astype(jnp.int32)
    index = jnp.concatenate([jnp.stack([left, b, right], axis=1), mine, ends], axis=1)
    meta = jnp.stack([core, span, half]).astype(jnp.int32)

    stats = jnp.stack([row_lse.reshape(2, HALF, BLOCK), row_delta.reshape(2, HALF, BLOCK)], axis=1)
    memory = jnp.stack([memory_keys, memory_values])
    q, do, own, other, far, far_other, stats, memory = gather_call(
        sends, queries, grad_out, keys, values, stats, memory
    )
    gq, keep, give, dmem = attend_call(meta, index, q, do, stats, own, other, far, far_other, memory)
    total, back, part = give_back_call(keep, give, dmem.reshape(PARTS, ROWS, FEATURES))
    here, away = settle_call(meta, sends, total, back)
    gq, dk, dv, mem = deliver_call(gq, here, away, part)
    mem = mem.reshape(2, BLOCK, FEATURES)
    return gq, dk, dv, mem[0], mem[1]


def solution(mesh):
    tokens = P(("blk", "uly"), None)
    heads = P(None, "uly")
    return jax.shard_map(
        shards,
        mesh=mesh,
        in_specs=(tokens, tokens, tokens, tokens, P("blk", "uly"), P("blk", "uly"), P(), heads, heads),
        out_specs=(tokens, tokens, tokens, heads, heads),
        check_vma=False,
    )
```

```python
import functools

import jax
import jax.numpy as jnp
from jax import lax
from jax.experimental import pallas as pl
from jax.experimental.pallas import tpu as pltpu
from jax.sharding import PartitionSpec as P

QUERY_HEADS = 32
KEY_HEADS = 8
FEATURES = 128
BLOCK = 128
RANDOM = 2
SLOTS = 3 + RANDOM
SCALE = FEATURES ** (-0.5)
MESH = pl.DeviceIdType.MESH

SPANS, PLACES = 24, 32
HALF = PLACES // 2
YS = HALF // 2
X, Z = 4, 6
PARTS = 8
ROWS = 4 * BLOCK // PARTS

F32, BF16 = jnp.float32, jnp.bfloat16


def position():
    s, u = lax.axis_index("blk"), lax.axis_index("uly")
    return s, u, u // HALF, u % HALF, u % 2


def far_peers(s, u, body):
    x, a = s % X, s // X
    half, p = u // HALF, u % HALF
    odd = x % 2

    def along(step):
        lo = a + step
        crossed = (lo < 0) | (lo >= Z)
        lo = jnp.where(lo < 0, lo + Z, jnp.where(lo >= Z, lo - Z, lo))
        return lo * X, jnp.where(crossed, 1 - half, half) * HALF + p

    for step in (0, 1, -1, 2, -2):
        base, place = along(step)
        for xx in range(X):
            if step:
                body(base + xx, place)
            else:
                pl.when(x != xx)(functools.partial(body, base + xx, place))
    base = jnp.where(a < Z // 2, a + Z // 2, a - Z // 2) * X
    within, across = half * HALF + p, (1 - half) * HALF + p
    even_place = jnp.where(odd == 0, within, across)
    odd_place = jnp.where(odd == 0, across, within)
    for xx in range(X):
        body(base + xx, odd_place if xx % 2 else even_place)


def remote(src, dst, sent, got, blk, uly):
    return pltpu.make_async_remote_copy(
        src_ref=src, dst_ref=dst, send_sem=sent, recv_sem=got, device_id=(blk, uly), device_id_type=MESH
    )


def send(src, dst, sent, got, blk, uly, here):
    @pl.when(jnp.logical_not(here))
    def _():
        remote(src, dst, sent, got, blk, uly).start()

    @pl.when(here)
    def _():
        pltpu.make_async_copy(src, dst, got).start()


def wait(ref, sem):
    pltpu.make_async_copy(ref, ref, sem).wait()


def loop(n, body):
    def step(i, carry):
        body(i)
        return carry

    lax.fori_loop(0, n, step, 0)


def greet(blk, uly):
    pl.semaphore_signal(pltpu.get_barrier_semaphore(), inc=1, device_id=(blk, uly), device_id_type=MESH)


def others(n, me, body):
    def step(i):
        @pl.when(i != me)
        def _():
            body(i)

    loop(n, step)


def part_peer(s, r):
    return ((s // X) // 2 * 2 + r % 2) * X + r // 2


def my_part(s):
    return s % X * 2 + s // X % 2


ENTRIES = HALF * RANDOM
NEAR = HALF + 2
ZERO = ENTRIES + NEAR
CHUNK = 8
MIDDLE = 8


def attend(
    send_ref, entry_ref, named_ref, q_ref, do_ref, k_ref, v_ref, lse_ref, delta_ref, mk_ref, mv_ref,
    gq_ref, sum_ref, back_ref, part_ref,
    qh_ref, doh_ref, own_ref, far_ref, out_ref, pool_ref, terms_ref, got_ref, dq_ref, near_ref, macc_ref,
    stat_ref, mem_ref, dmem_ref, parts_ref,
    s_kv, r_kv, s_q, r_q, s_do, r_do, s_z, r_z, s_core, r_core, c_own, s_far, r_far, s_back, r_back,
    s_stat, r_stat, s_mem, r_mem, s_term, r_term, s_part, r_part,
):
    s, u, half, p_me, core = position()
    y, first = p_me // 2, half * HALF
    second = HALF - first
    core_peer = u + 1 - 2 * core
    r_me = my_part(s)
    others(PLACES, u, lambda p: greet(s, p))
    far_peers(s, u, greet)
    others(PARTS, r_me, lambda r: greet(part_peer(s, r), u))
    pl.semaphore_wait(pltpu.get_barrier_semaphore(), PLACES - 1 + SPANS - 1 + PARTS - 1)

    def columns(ref, i, width):
        return ref.at[:, pl.ds(pl.multiple_of(i * width, width), width)]

    def nearest(n):
        k = (n + 1) // 2
        return (y + jnp.where(n % 2 == 1, k, YS - k)) % YS

    def kv_to(n):
        to = nearest(n)
        for kind, ref in ((0, k_ref), (1, v_ref)):
            place = first + 2 * to + kind
            send(columns(ref, to, FEATURES), own_ref.at[first + p_me], s_kv, r_kv.at[y], s, place, place == u)

    loop(YS, kv_to)
    for z in range(2):
        place = z * HALF + u // 2
        for kind, stat, mem in ((0, lse_ref, mk_ref), (1, delta_ref, mv_ref)):
            send(stat.at[z], stat_ref.at[u % 2, kind], s_stat.at[z, kind], r_stat, s, place, place == u)
            send(mem, mem_ref.at[u % 2, kind], s_mem.at[z, kind], r_mem, s, place, place == u)

    def q_to(n):
        p = 2 * nearest(n // 2) + n % 2
        here = p == p_me
        send(columns(q_ref, p, 2 * FEATURES), qh_ref.at[p_me], s_q, r_q.at[p_me], s, first + p, here)
        send(columns(do_ref, p, 2 * FEATURES), doh_ref.at[p_me], s_do, r_do.at[p_me], s, first + p, here)

    loop(HALF, q_to)
    near_ref[...] = jnp.zeros_like(near_ref)
    macc_ref[...] = jnp.zeros_like(macc_ref)
    for kind in range(2):
        terms_ref[kind, ZERO] = jnp.zeros((BLOCK, FEATURES), BF16)
    got_ref[ZERO] = jnp.zeros((BLOCK, FEATURES), BF16)

    def kv_on(n):
        at = pl.ds(first + 2 * nearest(n), 2)
        piece = own_ref.at[at]
        wait(piece, r_kv.at[nearest(n)])
        remote(piece, piece, s_z, r_z, s, (u + HALF) % PLACES).start()
        remote(piece, pool_ref.at[core, at], s_core.at[0], r_core.at[0], s, core_peer).start()
        pltpu.make_async_copy(piece, pool_ref.at[core, at], c_own.at[0]).start()

    loop(YS, kv_on)
    mine, theirs = pl.ds(first, HALF), pl.ds(second, HALF)
    wait(pool_ref.at[core, mine], c_own.at[0])
    wait(pool_ref.at[1 - core, mine], r_core.at[0])
    wait(stat_ref, r_stat)
    wait(mem_ref, r_mem)

    def dot(a, b, i, j):
        return lax.dot_general(a, b, (((i,), (j,)), ((), ())), preferred_element_type=F32)

    def block(j):
        q = [qh_ref[j, :, FEATURES * i : FEATURES * (i + 1)] for i in range(2)]
        do = [doh_ref[j, :, FEATURES * i : FEATURES * (i + 1)] for i in range(2)]
        lse, delta = [
            jnp.concatenate([stat_ref[i, kind, pl.ds(j, 1), :] for i in range(2)], axis=1) for kind in range(2)
        ]
        return q, do, lse, delta

    def pairs(keys, values, q2, do2, lse, delta, okay=None):
        weights = jnp.exp(dot(keys, q2, 1, 1) * SCALE - lse)
        dscores = weights * (dot(values, do2, 1, 1) - delta)
        if okay is not None:
            weights, dscores = jnp.where(okay, weights, 0.0), jnp.where(okay, dscores, 0.0)
        weight_bf, dscore_bf = weights.astype(BF16), dscores.astype(BF16)
        return dot(dscore_bf, q2, 1, 0) * SCALE, dot(weight_bf, do2, 1, 0), dot(dscore_bf, keys, 0, 0)

    def at_once(j):
        wait(qh_ref.at[j], r_q.at[j])
        wait(doh_ref.at[j], r_do.at[j])
        q, do, lse, delta = block(j)
        for i in range(2):
            cols = slice(FEATURES * i, FEATURES * (i + 1))
            dk, dv, dq = pairs(mem_ref[i, 0], mem_ref[i, 1], q[i], do[i], lse[:, cols], delta[:, cols])
            macc_ref[i, 0] += dk
            macc_ref[i, 1] += dv
            dq_ref[j, BLOCK * i : BLOCK * (i + 1)] = dq

        @pl.when((j > 0) & (j < HALF - 1))
        def _():
            at = pl.ds(first + j - 1, 3)
            keys = pool_ref[0, at].reshape(3 * BLOCK, FEATURES)
            values = pool_ref[1, at].reshape(3 * BLOCK, FEATURES)
            q2, do2 = jnp.concatenate(q, axis=0), jnp.concatenate(do, axis=0)
            dk, dv, dq = pairs(keys, values, q2, do2, lse, delta)
            near_ref[0, pl.ds(j, 3)] += dk.reshape(3, BLOCK, FEATURES)
            near_ref[1, pl.ds(j, 3)] += dv.reshape(3, BLOCK, FEATURES)
            dq_ref[j] += dq

    def in_order(n):
        at_once(2 * nearest(n // 2) + n % 2)

    loop(MIDDLE, in_order)
    wait(own_ref.at[theirs], r_z)
    onward = remote(own_ref.at[theirs], pool_ref.at[core, theirs], s_core.at[1], r_core.at[1], s, core_peer)
    onward.start()
    pltpu.make_async_copy(own_ref.at[theirs], pool_ref.at[core, theirs], c_own.at[1]).start()

    def far_to(t, place):
        out_ref[t] = own_ref[send_ref[t]]
        remote(out_ref.at[t], far_ref.at[s], s_far, r_far, t, place).start()

    far_peers(s, u, far_to)
    loop(HALF - MIDDLE, lambda n: in_order(n + MIDDLE))

    for i in range(2):
        for kind in range(2):
            for n in range(BLOCK // ROWS):
                dmem_ref[i * 4 + kind * 2 + n] = macc_ref[i, kind, ROWS * n : ROWS * (n + 1)]

    def part_to(r):
        remote(dmem_ref.at[r], parts_ref.at[r_me], s_part, r_part, part_peer(s, r), u).start()

    others(PARTS, r_me, part_to)
    rest = pl.ds(0, SPANS - 1)
    far_at = pl.ds(PLACES, SPANS)
    wait(far_ref.at[rest], r_far)
    onward_far = remote(far_ref, pool_ref.at[core, far_at], s_core.at[2], r_core.at[2], s, core_peer)
    onward_far.start()
    pltpu.make_async_copy(far_ref, pool_ref.at[core, far_at], c_own.at[2]).start()
    wait(out_ref.at[rest], s_far)
    for n, at in ((1, theirs), (2, far_at)):
        wait(pool_ref.at[core, at], c_own.at[n])
        wait(pool_ref.at[1 - core, at], r_core.at[n])

    left_okay = (half > 0) | (s > 0)
    right_okay = (half == 0) | (s < SPANS - 1)
    left = jnp.where(half > 0, first - 1, jnp.where(s > 0, PLACES + s - 1, first))
    right = jnp.where(half == 0, HALF, jnp.where(s < SPANS - 1, PLACES + s + 1, first + HALF - 1))
    for j, outer, slot, okay in ((0, left, 0, left_okay), (HALF - 1, right, 2, right_okay)):
        q, do, lse, delta = block(j)
        q2, do2 = jnp.concatenate(q, axis=0), jnp.concatenate(do, axis=0)
        for n, where in ((slot, outer), (1, first + j), (2 - slot, first + (1 if slot == 0 else HALF - 2))):
            dk, dv, dq = pairs(
                pool_ref[0, where], pool_ref[1, where], q2, do2, lse, delta, okay if n == slot else None
            )
            near_ref[0, j + n] += dk
            near_ref[1, j + n] += dv
            dq_ref[j] += dq

    def near_to(n):
        for kind in range(2):
            terms_ref[kind, ENTRIES + n] = near_ref[kind, n].astype(BF16)

    loop(NEAR, near_to)
    chunks = ENTRIES // CHUNK

    def terms_to(n, start, count):
        at = pl.ds(start, count)
        return remote(terms_ref.at[1 - core, at], got_ref.at[at], s_term.at[n], r_term.at[n], s, core_peer)

    terms_to(chunks, ENTRIES, NEAR).start()

    def random(j):
        q, do, lse, delta = block(j)
        which = []
        for r in range(RANDOM):
            named = named_ref[j, r]
            which.append(jnp.where(named // PLACES == s, named % PLACES, PLACES + named // PLACES))
        keys = jnp.concatenate([pool_ref[0, w] for w in which], axis=0)
        values = jnp.concatenate([pool_ref[1, w] for w in which], axis=0)
        dk, dv, dq = pairs(
            keys, values, jnp.concatenate(q, axis=0), jnp.concatenate(do, axis=0), lse, delta
        )
        at = pl.ds(RANDOM * j, RANDOM)
        terms_ref[0, at] = dk.astype(BF16).reshape(RANDOM, BLOCK, FEATURES)
        terms_ref[1, at] = dv.astype(BF16).reshape(RANDOM, BLOCK, FEATURES)
        dq = (dq_ref[j] + dq) * SCALE
        for i in range(2):
            gq_ref[j, :, FEATURES * i : FEATURES * (i + 1)] = dq[BLOCK * i : BLOCK * (i + 1)].astype(BF16)
        per = CHUNK // RANDOM

        @pl.when(j % per == per - 1)
        def _():
            terms_to(j // per, j // per * CHUNK, CHUNK).start()

    loop(HALF, random)
    for n in range(chunks):
        terms_to(n, n * CHUNK, CHUNK).wait()
    terms_to(chunks, ENTRIES, NEAR).wait()

    def back_to(t, place):
        e = entry_ref[t]
        out_ref[t] = (terms_ref[core, e].astype(F32) + got_ref[e].astype(F32)).astype(BF16)
        remote(out_ref.at[t], back_ref.at[s], s_back, r_back, t, place).start()

    far_peers(s, u, back_to)

    def add(n):
        sum_ref[n] = (terms_ref[core, n].astype(F32) + got_ref[n].astype(F32)).astype(BF16)

    loop(ZERO, add)
    wait(parts_ref.at[pl.ds(0, PARTS - 1)], r_part)
    parts_ref[r_me] = dmem_ref[r_me]
    part_ref[...] = jnp.sum(parts_ref[...], axis=0)
    wait(back_ref.at[rest], r_back)
    wait(out_ref.at[rest], s_back)
    wait(parts_ref.at[pl.ds(0, PARTS - 1)], s_part)
    wait(own_ref.at[pl.ds(0, HALF - 1)], s_kv)
    wait(own_ref.at[mine], s_z)
    wait(own_ref.at[mine], s_core.at[0])
    onward.wait_send()
    onward_far.wait_send()
    wait(qh_ref.at[pl.ds(0, HALF - 1)], s_q)
    wait(doh_ref.at[pl.ds(0, HALF - 1)], s_do)
    for z in range(2):
        @pl.when(z * HALF + u // 2 != u)
        def _():
            for kind in range(2):
                wait(stat_ref.at[0, kind], s_stat.at[z, kind])
                wait(mem_ref.at[0, kind], s_mem.at[z, kind])


def vmem(n):
    return [pl.BlockSpec(memory_space=pltpu.VMEM)] * n


def hbm(n):
    return [pl.BlockSpec(memory_space=pl.ANY)] * n


SMEM = pl.BlockSpec(memory_space=pltpu.SMEM)
DMA = pltpu.SemaphoreType.DMA


def shape(*dims, dtype=BF16):
    return jax.ShapeDtypeStruct(dims, dtype)


def attend_call(sends, entries, named, q, do, k, v, lse, delta, mk, mv):
    tile = (BLOCK, FEATURES)
    wide = (HALF, BLOCK, 2 * FEATURES)
    one, per_kind = DMA, DMA((2, 2))
    return pl.pallas_call(
        attend,
        in_specs=[SMEM] * 3 + hbm(8),
        out_specs=vmem(4),
        out_shape=[shape(*wide), shape(ZERO, *tile), shape(SPANS, *tile), shape(ROWS, FEATURES, dtype=F32)],
        scratch_shapes=[
            pltpu.VMEM(wide, BF16),
            pltpu.VMEM(wide, BF16),
            pltpu.VMEM((PLACES,) + tile, BF16),
            pltpu.VMEM((SPANS,) + tile, BF16),
            pltpu.VMEM((SPANS,) + tile, BF16),
            pltpu.VMEM((2, PLACES + SPANS) + tile, BF16),
            pltpu.VMEM((2, ZERO + 1) + tile, BF16),
            pltpu.VMEM((ZERO + 1,) + tile, BF16),
            pltpu.VMEM((HALF, 2 * BLOCK, FEATURES), F32),
            pltpu.VMEM((2, NEAR) + tile, F32),
            pltpu.VMEM((2, 2) + tile, F32),
            pltpu.VMEM((2, 2, HALF, BLOCK), F32),
            pltpu.VMEM((2, 2) + tile, BF16),
            pltpu.VMEM((PARTS, ROWS, FEATURES), F32),
            pltpu.VMEM((PARTS, ROWS, FEATURES), F32),
            one, DMA((YS,)), one, DMA((HALF,)), one, DMA((HALF,)), one, one,
            DMA((3,)), DMA((3,)), DMA((3,)), one, one, one, one,
            per_kind, one, per_kind, one, DMA((5,)), DMA((5,)), one, one,
        ],
        compiler_params=pltpu.CompilerParams(collective_id=0, has_side_effects=True),
        name="attend",
    )(sends, entries, named, q, do, k, v, lse, delta, mk, mv)


def settle(meta_ref, send_ref, named_ref, sum_ref, back_ref, here_ref, away_ref, acc_ref):
    acc_ref[...] = jnp.zeros_like(acc_ref)
    s, half = meta_ref[0], meta_ref[1]

    @pl.loop(0, HALF)
    def _(j):
        for r in range(RANDOM):
            named = named_ref[j, r]

            @pl.when(named // PLACES == s)
            def _():
                acc_ref[named % PLACES] += sum_ref[RANDOM * j + r].astype(F32)

    @pl.loop(0, NEAR)
    def _(n):
        at = half * HALF - 1 + n

        @pl.when((at >= 0) & (at < PLACES))
        def _():
            acc_ref[at] += sum_ref[ENTRIES + n].astype(F32)

    @pl.loop(0, SPANS)
    def _(t):
        @pl.when(t != s)
        def _():
            acc_ref[send_ref[t]] += back_ref[t].astype(F32)

    @pl.loop(0, HALF)
    def _(n):
        here_ref[n] = acc_ref[half * HALF + n]
        away_ref[n] = acc_ref[(1 - half) * HALF + n].astype(BF16)


def settle_call(meta, sends, named, total, back):
    tile = (BLOCK, FEATURES)
    return pl.pallas_call(
        settle,
        in_specs=[SMEM] * 3 + vmem(2),
        out_specs=vmem(2),
        out_shape=[shape(HALF, *tile, dtype=F32), shape(HALF, *tile)],
        scratch_shapes=[pltpu.VMEM((PLACES,) + tile, F32)],
        name="settle",
    )(meta, sends, named, total, back)


CHUNKS = 4
RINGS = 6


def deliver(
    gq_ref, here_ref, away_ref, part_ref, gq_out, dk_ref, dv_ref, mk_out, mv_out,
    mem_out, got_ref, out_ref, rows_ref, parts_ref, sum_ref,
    s_z, r_z, s_q, r_q, s_rows, r_rows, s_part, r_part, s_mem, r_mem,
):
    s, u, half, p_me, core = position()
    first = half * HALF
    r_me = my_part(s)
    ring_me = (s // X) // 2 * 2 + half
    y = p_me // 2
    head = 4 * y + 2 * core + r_me // 4
    source = first + u // 2

    def ring_peer(r):
        return ((r // 2) * 2 + s // X % 2) * X + s % X, r % 2 * HALF + p_me

    gives = half == y // 4

    def takers(body):
        def step(r):
            blk = part_peer(s, r)

            @pl.when(jnp.logical_not((blk == s) & (head == u)))
            def _():
                body(r, blk)

        loop(PARTS, step)

    def givers(body):
        def step(n):
            blk = part_peer(s, u % 2 * 4 + n)

            @pl.when(jnp.logical_not((blk == s) & (source == u)))
            def _():
                body(blk)

        loop(4, step)

    others(HALF, p_me, lambda p: greet(s, first + p))
    greet(s, (u + HALF) % PLACES)
    others(RINGS, ring_me, lambda r: greet(*ring_peer(r)))

    @pl.when(gives)
    def _():
        takers(lambda r, blk: greet(blk, head))

    givers(lambda blk: greet(blk, source))
    own = ((r_me // 4 == u % 2) & (source == u)).astype(jnp.int32)
    count = HALF + RINGS - 1 + 4 - own + jnp.where(gives, PARTS - own, 0)
    pl.semaphore_wait(pltpu.get_barrier_semaphore(), count)

    def part_to(r):
        remote(part_ref, parts_ref.at[ring_me], s_part, r_part, *ring_peer(r)).start()

    others(RINGS, ring_me, part_to)
    each = HALF // CHUNKS
    swaps = []
    for n in range(CHUNKS):
        rows = pl.ds(n * each, each)
        swaps.append(remote(away_ref.at[rows], got_ref.at[rows], s_z.at[n], r_z.at[n], s, (u + HALF) % PLACES))
        swaps[-1].start()

    def columns(ref, i, width):
        return ref.at[:, pl.ds(pl.multiple_of(i * width, width), width)]

    def gq_to(p):
        send(gq_ref.at[p], columns(gq_out, p_me, 2 * FEATURES), s_q, r_q, s, first + p, p == p_me)

    loop(HALF, gq_to)
    for n in range(CHUNKS):
        swaps[n].wait_recv()

        def rows_to(i):
            p = n * each + i
            out_ref[p] = (here_ref[p] + got_ref[p].astype(F32)).astype(BF16)
            send(out_ref.at[p], rows_ref.at[p_me], s_rows, r_rows, s, first + p, p == p_me)

        loop(each, rows_to)
        if n == 0:
            wait(parts_ref.at[pl.ds(0, RINGS - 1)], r_part)
            parts_ref[ring_me] = part_ref[...]
            sum_ref[...] = jnp.sum(parts_ref[...], axis=0)

            def mem_to(r):
                blk = part_peer(s, r)
                send(sum_ref, mem_out.at[r_me % 4], s_mem.at[r], r_mem, blk, head, (blk == s) & (head == u))

            @pl.when(gives)
            def _():
                loop(PARTS, mem_to)
    wait(rows_ref, r_rows)
    for head_id in range(KEY_HEADS):
        cols = slice(FEATURES * head_id, FEATURES * (head_id + 1))
        dk_ref[:, cols] = rows_ref[2 * head_id].astype(F32)
        dv_ref[:, cols] = rows_ref[2 * head_id + 1].astype(F32)
    wait(mem_out, r_mem)
    for n in range(2):
        mk_out[ROWS * n : ROWS * (n + 1), :] = mem_out[n]
        mv_out[ROWS * n : ROWS * (n + 1), :] = mem_out[2 + n]
    wait(gq_out, r_q)
    wait(out_ref.at[pl.ds(0, HALF - 1)], s_rows)
    wait(gq_out.at[:, pl.ds(0, (HALF - 1) * 2 * FEATURES)], s_q)
    wait(parts_ref.at[pl.ds(0, RINGS - 1)], s_part)
    for n in range(CHUNKS):
        swaps[n].wait_send()

    @pl.when(gives)
    def _():
        takers(lambda r, blk: wait(sum_ref, s_mem.at[r]))


def deliver_call(gq, here, away, part):
    tile = (BLOCK, FEATURES)
    return pl.pallas_call(
        deliver,
        in_specs=hbm(1) + vmem(3),
        out_specs=hbm(1) + vmem(4),
        out_shape=[
            shape(BLOCK, QUERY_HEADS * FEATURES),
            shape(BLOCK, KEY_HEADS * FEATURES, dtype=F32), shape(BLOCK, KEY_HEADS * FEATURES, dtype=F32),
            shape(BLOCK, FEATURES, dtype=F32), shape(BLOCK, FEATURES, dtype=F32),
        ],
        scratch_shapes=[
            pltpu.VMEM((4, ROWS, FEATURES), F32),
            pltpu.VMEM((HALF,) + tile, BF16), pltpu.VMEM((HALF,) + tile, BF16), pltpu.VMEM((HALF,) + tile, BF16),
            pltpu.VMEM((RINGS, ROWS, FEATURES), F32), pltpu.VMEM((ROWS, FEATURES), F32),
            DMA((CHUNKS,)), DMA((CHUNKS,)), DMA, DMA, DMA, DMA, DMA, DMA, DMA((PARTS,)), DMA,
        ],
        compiler_params=pltpu.CompilerParams(collective_id=2, has_side_effects=True),
        name="deliver",
    )(gq, here, away, part)


def shards(queries, keys, values, grad_out, row_lse, row_delta, pattern, memory_keys, memory_values):
    span, place = lax.axis_index("blk"), lax.axis_index("uly")
    half = place // HALF
    flat = pattern.reshape(SPANS, PLACES * RANDOM)
    ids = jnp.arange(SPANS, dtype=jnp.int32)
    from_me = (flat // PLACES == span) & (ids != span)[:, None]
    read = jnp.sum(jnp.where(from_me, flat % PLACES, 0), axis=1)
    sends = jnp.where(jnp.abs(ids - span) == 1, jnp.where(ids > span, PLACES - 1, 0), read)
    named = lax.dynamic_slice(pattern, (span * PLACES + half * HALF, 0), (HALF, RANDOM))
    number = jnp.arange(ENTRIES, dtype=jnp.int32).reshape(1, HALF, RANDOM)
    names = (named // PLACES)[None] == ids[:, None, None]
    entries = ZERO + jnp.sum(jnp.where(names, number - ZERO, 0), axis=(1, 2))
    entries = jnp.where((ids == span - 1) & (half == 0), ENTRIES, entries)
    entries = jnp.where((ids == span + 1) & (half == 1), ENTRIES + NEAR - 1, entries)
    meta = jnp.stack([span, half]).astype(jnp.int32)

    rows = (2, HALF, BLOCK)
    gq, total, back, part = attend_call(
        sends, entries, named, queries, grad_out, keys, values,
        row_lse.reshape(rows), row_delta.reshape(rows), memory_keys, memory_values,
    )
    here, away = settle_call(meta, sends, named, total, back)
    return tuple(deliver_call(gq, here, away, part))


def solution(mesh):
    tokens = P(("blk", "uly"), None)
    heads = P(None, "uly")
    return jax.shard_map(
        shards,
        mesh=mesh,
        in_specs=(tokens, tokens, tokens, tokens, P("blk", "uly"), P("blk", "uly"), P(), heads, heads),
        out_specs=(tokens, tokens, tokens, heads, heads),
        check_vma=False,
    )
```

```python
import functools

import jax
import jax.numpy as jnp
from jax import lax
from jax.experimental import pallas as pl
from jax.experimental.pallas import tpu as pltpu
from jax.sharding import PartitionSpec as P

QUERY_HEADS = 32
KEY_HEADS = 8
FEATURES = 128
BLOCK = 128
RANDOM = 2
SLOTS = 3 + RANDOM
SCALE = FEATURES ** (-0.5)
MESH = pl.DeviceIdType.MESH

SPANS, PLACES = 24, 32
HALF = PLACES // 2
YS = HALF // 2
X, Z = 4, 6
PARTS = 8
ROWS = 4 * BLOCK // PARTS

F32, BF16 = jnp.float32, jnp.bfloat16


def position():
    s, u = lax.axis_index("blk"), lax.axis_index("uly")
    return s, u, u // HALF, u % HALF, u % 2


def far_peers(s, u, body):
    x, a = s % X, s // X
    half, p = u // HALF, u % HALF
    odd = x % 2

    def along(step):
        lo = a + step
        crossed = (lo < 0) | (lo >= Z)
        lo = jnp.where(lo < 0, lo + Z, jnp.where(lo >= Z, lo - Z, lo))
        return lo * X, jnp.where(crossed, 1 - half, half) * HALF + p

    for step in (0, 1, -1, 2, -2):
        base, place = along(step)
        for xx in range(X):
            if step:
                body(base + xx, place)
            else:
                pl.when(x != xx)(functools.partial(body, base + xx, place))
    base = jnp.where(a < Z // 2, a + Z // 2, a - Z // 2) * X
    within, across = half * HALF + p, (1 - half) * HALF + p
    even_place = jnp.where(odd == 0, within, across)
    odd_place = jnp.where(odd == 0, across, within)
    for xx in range(X):
        body(base + xx, odd_place if xx % 2 else even_place)


def remote(src, dst, sent, got, blk, uly):
    return pltpu.make_async_remote_copy(
        src_ref=src, dst_ref=dst, send_sem=sent, recv_sem=got, device_id=(blk, uly), device_id_type=MESH
    )


def send(src, dst, sent, got, blk, uly, here):
    @pl.when(jnp.logical_not(here))
    def _():
        remote(src, dst, sent, got, blk, uly).start()

    @pl.when(here)
    def _():
        pltpu.make_async_copy(src, dst, got).start()


def wait(ref, sem):
    pltpu.make_async_copy(ref, ref, sem).wait()


def loop(n, body):
    def step(i, carry):
        body(i)
        return carry

    lax.fori_loop(0, n, step, 0)


def greet(blk, uly):
    pl.semaphore_signal(pltpu.get_barrier_semaphore(), inc=1, device_id=(blk, uly), device_id_type=MESH)


def others(n, me, body):
    def step(i):
        @pl.when(i != me)
        def _():
            body(i)

    loop(n, step)


def part_peer(s, r):
    return ((s // X) // 2 * 2 + r % 2) * X + r // 2


def my_part(s):
    return s % X * 2 + s // X % 2


ENTRIES = HALF * RANDOM
NEAR = HALF + 2
ZERO = ENTRIES + NEAR
LINKS = ENTRIES + SPANS
CHUNKS = 4
RINGS = 6
CHUNK = 8
MIDDLE = 8


def attend(
    send_ref, entry_ref, named_ref, before_ref, last_ref,
    q_ref, do_ref, k_ref, v_ref, lse_ref, delta_ref, mk_ref, mv_ref,
    gq_out, dk_ref, dv_ref, mk_out, mv_out,
    gq_ref, chain_ref, back_ref, part_ref, away_ref, came_ref, rows_out, rows_ref, rings_ref, total_ref, mem_out,
    qh_ref, doh_ref, own_ref, far_ref, out_ref, pool_ref, terms_ref, got_ref, dq_ref, near_ref, macc_ref,
    stat_ref, mem_ref, dmem_ref, parts_ref,
    s_kv, r_kv, s_q, r_q, s_do, r_do, s_z, r_z, s_core, r_core, c_own, s_far, r_far, s_back, r_back,
    s_stat, r_stat, s_mem, r_mem, s_term, r_term, s_part, r_part,
    s_gq, r_gq, s_away, r_away, s_rows, r_rows, s_ring, r_ring, s_out, r_out,
):
    s, u, half, p_me, core = position()
    y, first = p_me // 2, half * HALF
    second = HALF - first
    core_peer = u + 1 - 2 * core
    r_me = my_part(s)
    ring_me = (s // X) // 2 * 2 + half
    head = 4 * y + 2 * core + r_me // 4
    source = first + u // 2

    def ring_peer(r):
        return ((r // 2) * 2 + s // X % 2) * X + s % X, r % 2 * HALF + p_me

    gives = half == y // 4

    def takers(body):
        def step(r):
            blk = part_peer(s, r)

            @pl.when(jnp.logical_not((blk == s) & (head == u)))
            def _():
                body(r, blk)

        loop(PARTS, step)

    def givers(body):
        def step(n):
            blk = part_peer(s, u % 2 * 4 + n)

            @pl.when(jnp.logical_not((blk == s) & (source == u)))
            def _():
                body(blk)

        loop(4, step)

    others(PLACES, u, lambda p: greet(s, p))
    far_peers(s, u, greet)
    others(PARTS, r_me, lambda r: greet(part_peer(s, r), u))
    others(RINGS, ring_me, lambda r: greet(*ring_peer(r)))

    @pl.when(gives)
    def _():
        takers(lambda r, blk: greet(blk, head))

    givers(lambda blk: greet(blk, source))
    own = ((r_me // 4 == u % 2) & (source == u)).astype(jnp.int32)
    count = PLACES - 1 + SPANS - 1 + PARTS - 1 + RINGS - 1 + 4 - own + jnp.where(gives, PARTS - own, 0)
    pl.semaphore_wait(pltpu.get_barrier_semaphore(), count)

    def columns(ref, i, width):
        return ref.at[:, pl.ds(pl.multiple_of(i * width, width), width)]

    def nearest(n):
        k = (n + 1) // 2
        return (y + jnp.where(n % 2 == 1, k, YS - k)) % YS

    def kv_to(n):
        to = nearest(n)
        for kind, ref in ((0, k_ref), (1, v_ref)):
            place = first + 2 * to + kind
            send(columns(ref, to, FEATURES), own_ref.at[first + p_me], s_kv, r_kv.at[y], s, place, place == u)

    loop(YS, kv_to)
    for z in range(2):
        place = z * HALF + u // 2
        for kind, stat, mem in ((0, lse_ref, mk_ref), (1, delta_ref, mv_ref)):
            send(stat.at[z], stat_ref.at[u % 2, kind], s_stat.at[z, kind], r_stat, s, place, place == u)
            send(mem, mem_ref.at[u % 2, kind], s_mem.at[z, kind], r_mem, s, place, place == u)

    def q_to(n):
        p = 2 * nearest(n // 2) + n % 2
        here = p == p_me
        send(columns(q_ref, p, 2 * FEATURES), qh_ref.at[p_me], s_q, r_q.at[p_me], s, first + p, here)
        send(columns(do_ref, p, 2 * FEATURES), doh_ref.at[p_me], s_do, r_do.at[p_me], s, first + p, here)

    loop(HALF, q_to)
    near_ref[...] = jnp.zeros_like(near_ref)
    macc_ref[...] = jnp.zeros_like(macc_ref)
    for kind in range(2):
        terms_ref[kind, ZERO] = jnp.zeros((BLOCK, FEATURES), BF16)
    got_ref[ZERO] = jnp.zeros((BLOCK, FEATURES), BF16)
    chain_ref[LINKS] = jnp.zeros((BLOCK, FEATURES), F32)

    def kv_on(n):
        at = pl.ds(first + 2 * nearest(n), 2)
        piece = own_ref.at[at]
        wait(piece, r_kv.at[nearest(n)])
        remote(piece, piece, s_z, r_z, s, (u + HALF) % PLACES).start()
        remote(piece, pool_ref.at[core, at], s_core.at[0], r_core.at[0], s, core_peer).start()
        pltpu.make_async_copy(piece, pool_ref.at[core, at], c_own.at[0]).start()

    loop(YS, kv_on)
    mine, theirs = pl.ds(first, HALF), pl.ds(second, HALF)
    wait(pool_ref.at[core, mine], c_own.at[0])
    wait(pool_ref.at[1 - core, mine], r_core.at[0])
    wait(stat_ref, r_stat)
    wait(mem_ref, r_mem)

    def dot(a, b, i, j):
        return lax.dot_general(a, b, (((i,), (j,)), ((), ())), preferred_element_type=F32)

    def block(j):
        q = [qh_ref[j, :, FEATURES * i : FEATURES * (i + 1)] for i in range(2)]
        do = [doh_ref[j, :, FEATURES * i : FEATURES * (i + 1)] for i in range(2)]
        lse, delta = [
            jnp.concatenate([stat_ref[i, kind, pl.ds(j, 1), :] for i in range(2)], axis=1) for kind in range(2)
        ]
        return q, do, lse, delta

    def pairs(keys, values, q2, do2, lse, delta, okay=None):
        weights = jnp.exp(dot(keys, q2, 1, 1) * SCALE - lse)
        dscores = weights * (dot(values, do2, 1, 1) - delta)
        if okay is not None:
            weights, dscores = jnp.where(okay, weights, 0.0), jnp.where(okay, dscores, 0.0)
        weight_bf, dscore_bf = weights.astype(BF16), dscores.astype(BF16)
        return dot(dscore_bf, q2, 1, 0) * SCALE, dot(weight_bf, do2, 1, 0), dot(dscore_bf, keys, 0, 0)

    def at_once(j):
        wait(qh_ref.at[j], r_q.at[j])
        wait(doh_ref.at[j], r_do.at[j])
        q, do, lse, delta = block(j)
        for i in range(2):
            cols = slice(FEATURES * i, FEATURES * (i + 1))
            dk, dv, dq = pairs(mem_ref[i, 0], mem_ref[i, 1], q[i], do[i], lse[:, cols], delta[:, cols])
            macc_ref[i, 0] += dk
            macc_ref[i, 1] += dv
            dq_ref[j, BLOCK * i : BLOCK * (i + 1)] = dq

        @pl.when((j > 0) & (j < HALF - 1))
        def _():
            at = pl.ds(first + j - 1, 3)
            keys = pool_ref[0, at].reshape(3 * BLOCK, FEATURES)
            values = pool_ref[1, at].reshape(3 * BLOCK, FEATURES)
            q2, do2 = jnp.concatenate(q, axis=0), jnp.concatenate(do, axis=0)
            dk, dv, dq = pairs(keys, values, q2, do2, lse, delta)
            near_ref[0, pl.ds(j, 3)] += dk.reshape(3, BLOCK, FEATURES)
            near_ref[1, pl.ds(j, 3)] += dv.reshape(3, BLOCK, FEATURES)
            dq_ref[j] += dq

    def in_order(n):
        at_once(2 * nearest(n // 2) + n % 2)

    loop(MIDDLE, in_order)
    wait(own_ref.at[theirs], r_z)
    onward = remote(own_ref.at[theirs], pool_ref.at[core, theirs], s_core.at[1], r_core.at[1], s, core_peer)
    onward.start()
    pltpu.make_async_copy(own_ref.at[theirs], pool_ref.at[core, theirs], c_own.at[1]).start()

    def far_to(t, place):
        out_ref[t] = own_ref[send_ref[t]]
        remote(out_ref.at[t], far_ref.at[s], s_far, r_far, t, place).start()

    far_peers(s, u, far_to)
    loop(HALF - MIDDLE, lambda n: in_order(n + MIDDLE))

    for i in range(2):
        for kind in range(2):
            for n in range(BLOCK // ROWS):
                dmem_ref[i * 4 + kind * 2 + n] = macc_ref[i, kind, ROWS * n : ROWS * (n + 1)]

    def part_to(r):
        remote(dmem_ref.at[r], parts_ref.at[r_me], s_part, r_part, part_peer(s, r), u).start()

    others(PARTS, r_me, part_to)
    rest = pl.ds(0, SPANS - 1)
    far_at = pl.ds(PLACES, SPANS)
    wait(far_ref.at[rest], r_far)
    onward_far = remote(far_ref, pool_ref.at[core, far_at], s_core.at[2], r_core.at[2], s, core_peer)
    onward_far.start()
    pltpu.make_async_copy(far_ref, pool_ref.at[core, far_at], c_own.at[2]).start()
    wait(out_ref.at[rest], s_far)
    for n, at in ((1, theirs), (2, far_at)):
        wait(pool_ref.at[core, at], c_own.at[n])
        wait(pool_ref.at[1 - core, at], r_core.at[n])

    left_okay = (half > 0) | (s > 0)
    right_okay = (half == 0) | (s < SPANS - 1)
    left = jnp.where(half > 0, first - 1, jnp.where(s > 0, PLACES + s - 1, first))
    right = jnp.where(half == 0, HALF, jnp.where(s < SPANS - 1, PLACES + s + 1, first + HALF - 1))
    for j, outer, slot, okay in ((0, left, 0, left_okay), (HALF - 1, right, 2, right_okay)):
        q, do, lse, delta = block(j)
        q2, do2 = jnp.concatenate(q, axis=0), jnp.concatenate(do, axis=0)
        for n, where in ((slot, outer), (1, first + j), (2 - slot, first + (1 if slot == 0 else HALF - 2))):
            dk, dv, dq = pairs(
                pool_ref[0, where], pool_ref[1, where], q2, do2, lse, delta, okay if n == slot else None
            )
            near_ref[0, j + n] += dk
            near_ref[1, j + n] += dv
            dq_ref[j] += dq

    def near_to(n):
        for kind in range(2):
            terms_ref[kind, ENTRIES + n] = near_ref[kind, n].astype(BF16)

    loop(NEAR, near_to)
    chunks = ENTRIES // CHUNK

    def terms_to(n, start, count):
        at = pl.ds(start, count)
        return remote(terms_ref.at[1 - core, at], got_ref.at[at], s_term.at[n], r_term.at[n], s, core_peer)

    terms_to(chunks, ENTRIES, NEAR).start()

    def random(j):
        q, do, lse, delta = block(j)
        which = []
        for r in range(RANDOM):
            named = named_ref[j, r]
            which.append(jnp.where(named // PLACES == s, named % PLACES, PLACES + named // PLACES))
        keys = jnp.concatenate([pool_ref[0, w] for w in which], axis=0)
        values = jnp.concatenate([pool_ref[1, w] for w in which], axis=0)
        dk, dv, dq = pairs(
            keys, values, jnp.concatenate(q, axis=0), jnp.concatenate(do, axis=0), lse, delta
        )
        at = pl.ds(RANDOM * j, RANDOM)
        terms_ref[0, at] = dk.astype(BF16).reshape(RANDOM, BLOCK, FEATURES)
        terms_ref[1, at] = dv.astype(BF16).reshape(RANDOM, BLOCK, FEATURES)
        dq = (dq_ref[j] + dq) * SCALE
        for i in range(2):
            gq_ref[j, :, FEATURES * i : FEATURES * (i + 1)] = dq[BLOCK * i : BLOCK * (i + 1)].astype(BF16)
        send(gq_ref.at[j], columns(gq_out, p_me, 2 * FEATURES), s_gq, r_gq, s, first + j, j == p_me)
        per = CHUNK // RANDOM

        @pl.when(j % per == per - 1)
        def _():
            terms_to(j // per, j // per * CHUNK, CHUNK).start()

    loop(HALF, random)
    for n in range(chunks):
        terms_to(n, n * CHUNK, CHUNK).wait()
    terms_to(chunks, ENTRIES, NEAR).wait()

    def back_to(t, place):
        e = entry_ref[t]
        out_ref[t] = (terms_ref[core, e].astype(F32) + got_ref[e].astype(F32)).astype(BF16)
        remote(out_ref.at[t], back_ref.at[s], s_back, r_back, t, place).start()

    far_peers(s, u, back_to)

    wait(parts_ref.at[pl.ds(0, PARTS - 1)], r_part)
    parts_ref[r_me] = dmem_ref[r_me]
    part_ref[...] = jnp.sum(parts_ref[...], axis=0)

    def ring_to(r):
        remote(part_ref, rings_ref.at[ring_me], s_ring, r_ring, *ring_peer(r)).start()

    others(RINGS, ring_me, ring_to)

    def both(n):
        return terms_ref[core, n].astype(F32) + got_ref[n].astype(F32)

    def link(n):
        chain_ref[n] = both(n) + chain_ref[before_ref[n]]

    loop(ENTRIES, link)
    wait(back_ref.at[rest], r_back)

    def link_back(t):
        chain_ref[ENTRIES + t] = back_ref[t].astype(F32) + chain_ref[before_ref[ENTRIES + t]]

    others(SPANS, s, link_back)
    each = HALF // CHUNKS
    swaps = []
    beside, edge = jnp.where(half == 0, 0, HALF - 1), jnp.where(half == 0, NEAR - 1, 0)

    def away(n):
        met = jnp.where(n == beside, both(ENTRIES + edge), 0.0)
        away_ref[n] = (chain_ref[last_ref[second + n]] + met).astype(BF16)

    for c in range(CHUNKS):
        loop(each, lambda i: away(c * each + i))
        at = pl.ds(c * each, each)
        swaps.append(remote(away_ref.at[at], came_ref.at[at], s_away.at[c], r_away.at[c], s, (u + HALF) % PLACES))
        swaps[-1].start()

    wait(rings_ref.at[pl.ds(0, RINGS - 1)], r_ring)
    rings_ref[ring_me] = part_ref[...]
    total_ref[...] = jnp.sum(rings_ref[...], axis=0)

    def mem_to(r):
        blk = part_peer(s, r)
        send(total_ref, mem_out.at[r_me % 4], s_out.at[r], r_out, blk, head, (blk == s) & (head == u))

    @pl.when(gives)
    def _():
        loop(PARTS, mem_to)

    for c in range(CHUNKS):
        swaps[c].wait_recv()

        def rows_to(i):
            p = c * each + i
            here = chain_ref[last_ref[first + p]] + both(ENTRIES + 1 + p)
            rows_out[p] = (here + came_ref[p].astype(F32)).astype(BF16)
            send(rows_out.at[p], rows_ref.at[p_me], s_rows, r_rows, s, first + p, p == p_me)

        loop(each, rows_to)
    wait(mem_out, r_out)
    for n in range(2):
        mk_out[ROWS * n : ROWS * (n + 1), :] = mem_out[n]
        mv_out[ROWS * n : ROWS * (n + 1), :] = mem_out[2 + n]
    wait(rows_ref, r_rows)
    for head_id in range(KEY_HEADS):
        cols = slice(FEATURES * head_id, FEATURES * (head_id + 1))
        dk_ref[:, cols] = rows_ref[2 * head_id].astype(F32)
        dv_ref[:, cols] = rows_ref[2 * head_id + 1].astype(F32)
    wait(gq_out, r_gq)
    wait(rows_out.at[pl.ds(0, HALF - 1)], s_rows)
    wait(gq_ref.at[pl.ds(0, HALF - 1)], s_gq)
    wait(rings_ref.at[pl.ds(0, RINGS - 1)], s_ring)
    for c in range(CHUNKS):
        swaps[c].wait_send()

    @pl.when(gives)
    def _():
        takers(lambda r, blk: wait(total_ref, s_out.at[r]))

    wait(out_ref.at[rest], s_back)
    wait(parts_ref.at[pl.ds(0, PARTS - 1)], s_part)
    wait(own_ref.at[pl.ds(0, HALF - 1)], s_kv)
    wait(own_ref.at[mine], s_z)
    wait(own_ref.at[mine], s_core.at[0])
    onward.wait_send()
    onward_far.wait_send()
    wait(qh_ref.at[pl.ds(0, HALF - 1)], s_q)
    wait(doh_ref.at[pl.ds(0, HALF - 1)], s_do)
    for z in range(2):
        @pl.when(z * HALF + u // 2 != u)
        def _():
            for kind in range(2):
                wait(stat_ref.at[0, kind], s_stat.at[z, kind])
                wait(mem_ref.at[0, kind], s_mem.at[z, kind])


def vmem(n):
    return [pl.BlockSpec(memory_space=pltpu.VMEM)] * n


def hbm(n):
    return [pl.BlockSpec(memory_space=pl.ANY)] * n


SMEM = pl.BlockSpec(memory_space=pltpu.SMEM)
DMA = pltpu.SemaphoreType.DMA


def shape(*dims, dtype=BF16):
    return jax.ShapeDtypeStruct(dims, dtype)


def attend_call(sends, entries, named, before, last, q, do, k, v, lse, delta, mk, mv):
    tile = (BLOCK, FEATURES)
    wide = (HALF, BLOCK, 2 * FEATURES)
    one, per_kind = DMA, DMA((2, 2))
    return pl.pallas_call(
        attend,
        in_specs=[SMEM] * 5 + hbm(8),
        out_specs=hbm(1) + vmem(4),
        out_shape=[shape(BLOCK, QUERY_HEADS * FEATURES)]
        + [shape(BLOCK, KEY_HEADS * FEATURES, dtype=F32)] * 2
        + [shape(BLOCK, FEATURES, dtype=F32)] * 2,
        scratch_shapes=[
            pltpu.VMEM(wide, BF16),
            pltpu.VMEM((LINKS + 1,) + tile, F32),
            pltpu.VMEM((SPANS,) + tile, BF16),
            pltpu.VMEM((ROWS, FEATURES), F32),
            pltpu.VMEM((HALF,) + tile, BF16),
            pltpu.VMEM((HALF,) + tile, BF16),
            pltpu.VMEM((HALF,) + tile, BF16),
            pltpu.VMEM((HALF,) + tile, BF16),
            pltpu.VMEM((RINGS, ROWS, FEATURES), F32),
            pltpu.VMEM((ROWS, FEATURES), F32),
            pltpu.VMEM((4, ROWS, FEATURES), F32),
            pltpu.VMEM(wide, BF16),
            pltpu.VMEM(wide, BF16),
            pltpu.VMEM((PLACES,) + tile, BF16),
            pltpu.VMEM((SPANS,) + tile, BF16),
            pltpu.VMEM((SPANS,) + tile, BF16),
            pltpu.VMEM((2, PLACES + SPANS) + tile, BF16),
            pltpu.VMEM((2, ZERO + 1) + tile, BF16),
            pltpu.VMEM((ZERO + 1,) + tile, BF16),
            pltpu.VMEM((HALF, 2 * BLOCK, FEATURES), F32),
            pltpu.VMEM((2, NEAR) + tile, F32),
            pltpu.VMEM((2, 2) + tile, F32),
            pltpu.VMEM((2, 2, HALF, BLOCK), F32),
            pltpu.VMEM((2, 2) + tile, BF16),
            pltpu.VMEM((PARTS, ROWS, FEATURES), F32),
            pltpu.VMEM((PARTS, ROWS, FEATURES), F32),
            one, DMA((YS,)), one, DMA((HALF,)), one, DMA((HALF,)), one, one,
            DMA((3,)), DMA((3,)), DMA((3,)), one, one, one, one,
            per_kind, one, per_kind, one, DMA((5,)), DMA((5,)), one, one,
            one, one, DMA((CHUNKS,)), DMA((CHUNKS,)), one, one, one, one, DMA((PARTS,)), one,
        ],
        compiler_params=pltpu.CompilerParams(collective_id=0, has_side_effects=True),
        name="attend",
    )(sends, entries, named, before, last, q, do, k, v, lse, delta, mk, mv)


def shards(queries, keys, values, grad_out, row_lse, row_delta, pattern, memory_keys, memory_values):
    span, place = lax.axis_index("blk"), lax.axis_index("uly")
    half = place // HALF
    flat = pattern.reshape(SPANS, PLACES * RANDOM)
    ids = jnp.arange(SPANS, dtype=jnp.int32)
    from_me = (flat // PLACES == span) & (ids != span)[:, None]
    read = jnp.sum(jnp.where(from_me, flat % PLACES, 0), axis=1)
    sends = jnp.where(jnp.abs(ids - span) == 1, jnp.where(ids > span, PLACES - 1, 0), read)
    named = lax.dynamic_slice(pattern, (span * PLACES + half * HALF, 0), (HALF, RANDOM))
    number = jnp.arange(ENTRIES, dtype=jnp.int32).reshape(1, HALF, RANDOM)
    names = (named // PLACES)[None] == ids[:, None, None]
    entries = ZERO + jnp.sum(jnp.where(names, number - ZERO, 0), axis=(1, 2))
    entries = jnp.where((ids == span - 1) & (half == 0), ENTRIES, entries)
    entries = jnp.where((ids == span + 1) & (half == 1), ENTRIES + NEAR - 1, entries)
    links = jnp.arange(LINKS, dtype=jnp.int32)
    blocks = jnp.concatenate(
        [jnp.where(named // PLACES == span, named % PLACES, -1).reshape(ENTRIES), jnp.where(ids == span, -1, sends)]
    )
    earlier = (blocks[:, None] == blocks[None]) & (links[:, None] > links[None])
    before = jnp.max(jnp.where(earlier, links[None], -1), axis=1)
    before = jnp.where(before < 0, LINKS, before)
    naming = blocks[None] == jnp.arange(PLACES, dtype=jnp.int32)[:, None]
    last = jnp.max(jnp.where(naming, links[None], -1), axis=1)
    last = jnp.where(last < 0, LINKS, last)

    rows = (2, HALF, BLOCK)
    return tuple(attend_call(
        sends, entries, named, before, last, queries, grad_out, keys, values,
        row_lse.reshape(rows), row_delta.reshape(rows), memory_keys, memory_values,
    ))


def solution(mesh):
    tokens = P(("blk", "uly"), None)
    heads = P(None, "uly")
    return jax.shard_map(
        shards,
        mesh=mesh,
        in_specs=(tokens, tokens, tokens, tokens, P("blk", "uly"), P("blk", "uly"), P(), heads, heads),
        out_specs=(tokens, tokens, tokens, heads, heads),
        check_vma=False,
    )
```

```python
import functools

import jax
import jax.numpy as jnp
from jax import lax
from jax.experimental import pallas as pl
from jax.experimental.pallas import tpu as pltpu
from jax.sharding import PartitionSpec as P

QUERY_HEADS = 32
KEY_HEADS = 8
FEATURES = 128
BLOCK = 128
RANDOM = 2
SLOTS = 3 + RANDOM
SCALE = FEATURES ** (-0.5)
MESH = pl.DeviceIdType.MESH

SPANS, PLACES = 24, 32
HALF = PLACES // 2
YS = HALF // 2
X, Z = 4, 6
PARTS = 8
ROWS = 4 * BLOCK // PARTS

F32, BF16 = jnp.float32, jnp.bfloat16


def position():
    s, u = lax.axis_index("blk"), lax.axis_index("uly")
    return s, u, u // HALF, u % HALF, u % 2


def far_peers(s, u, body):
    x, a = s % X, s // X
    half, p = u // HALF, u % HALF
    odd = x % 2

    def along(step):
        lo = a + step
        crossed = (lo < 0) | (lo >= Z)
        lo = jnp.where(lo < 0, lo + Z, jnp.where(lo >= Z, lo - Z, lo))
        return lo * X, jnp.where(crossed, 1 - half, half) * HALF + p

    for step in (0, 1, -1, 2, -2):
        base, place = along(step)
        for xx in range(X):
            if step:
                body(base + xx, place)
            else:
                pl.when(x != xx)(functools.partial(body, base + xx, place))
    base = jnp.where(a < Z // 2, a + Z // 2, a - Z // 2) * X
    within, across = half * HALF + p, (1 - half) * HALF + p
    even_place = jnp.where(odd == 0, within, across)
    odd_place = jnp.where(odd == 0, across, within)
    for xx in range(X):
        body(base + xx, odd_place if xx % 2 else even_place)


def remote(src, dst, sent, got, blk, uly):
    return pltpu.make_async_remote_copy(
        src_ref=src, dst_ref=dst, send_sem=sent, recv_sem=got, device_id=(blk, uly), device_id_type=MESH
    )


def send(src, dst, sent, got, blk, uly, here):
    @pl.when(jnp.logical_not(here))
    def _():
        remote(src, dst, sent, got, blk, uly).start()

    @pl.when(here)
    def _():
        pltpu.make_async_copy(src, dst, got).start()


def wait(ref, sem):
    pltpu.make_async_copy(ref, ref, sem).wait()


def loop(n, body):
    def step(i, carry):
        body(i)
        return carry

    lax.fori_loop(0, n, step, 0)


def greet(blk, uly):
    pl.semaphore_signal(pltpu.get_barrier_semaphore(), inc=1, device_id=(blk, uly), device_id_type=MESH)


def others(n, me, body):
    def step(i):
        @pl.when(i != me)
        def _():
            body(i)

    loop(n, step)


def part_peer(s, r):
    return ((s // X) // 2 * 2 + r % 2) * X + r // 2


def my_part(s):
    return s % X * 2 + s // X % 2


ENTRIES = HALF * RANDOM
NEAR = HALF + 2
ZERO = ENTRIES + NEAR
LINKS = ENTRIES + SPANS
CHUNKS = 4
RINGS = 6
CHUNK = 8
MIDDLE = 8
LATE = 14


def attend(
    send_ref, entry_ref, named_ref, before_ref, last_ref,
    q_ref, do_ref, k_ref, v_ref, lse_ref, delta_ref, mk_ref, mv_ref,
    gq_out, rows_ref, mem_out,
    gq_ref, chain_ref, back_ref, part_ref, away_ref, came_ref, rows_out, rings_ref, total_ref,
    qh_ref, doh_ref, own_ref, far_ref, out_ref, pool_ref, terms_ref, got_ref, dq_ref, near_ref, macc_ref,
    stat_ref, mem_ref, dmem_ref, parts_ref,
    s_kv, r_kv, s_q, r_q, s_do, r_do, s_z, r_z, s_core, r_core, c_own, s_far, r_far, s_back, r_back,
    s_stat, r_stat, s_mem, r_mem, s_term, r_term, s_part, r_part,
    s_gq, r_gq, s_away, r_away, s_rows, r_rows, s_ring, r_ring, s_out, r_out,
):
    s, u, half, p_me, core = position()
    y, first = p_me // 2, half * HALF
    second = HALF - first
    core_peer = u + 1 - 2 * core
    r_me = my_part(s)
    ring_me = (s // X) // 2 * 2 + half
    head = 4 * y + 2 * core + r_me // 4
    source = first + u // 2

    def ring_peer(r):
        return ((r // 2) * 2 + s // X % 2) * X + s % X, r % 2 * HALF + p_me

    gives = half == y // 4

    def takers(body):
        def step(r):
            blk = part_peer(s, r)

            @pl.when(jnp.logical_not((blk == s) & (head == u)))
            def _():
                body(r, blk)

        loop(PARTS, step)

    def givers(body):
        def step(n):
            blk = part_peer(s, u % 2 * 4 + n)

            @pl.when(jnp.logical_not((blk == s) & (source == u)))
            def _():
                body(blk)

        loop(4, step)

    others(PLACES, u, lambda p: greet(s, p))
    far_peers(s, u, greet)
    others(PARTS, r_me, lambda r: greet(part_peer(s, r), u))
    others(RINGS, ring_me, lambda r: greet(*ring_peer(r)))

    @pl.when(gives)
    def _():
        takers(lambda r, blk: greet(blk, head))

    givers(lambda blk: greet(blk, source))
    own = ((r_me // 4 == u % 2) & (source == u)).astype(jnp.int32)
    count = PLACES - 1 + SPANS - 1 + PARTS - 1 + RINGS - 1 + 4 - own + jnp.where(gives, PARTS - own, 0)
    pl.semaphore_wait(pltpu.get_barrier_semaphore(), count)

    def columns(ref, i, width):
        return ref.at[:, pl.ds(pl.multiple_of(i * width, width), width)]

    def nearest(n):
        k = (n + 1) // 2
        return (y + jnp.where(n % 2 == 1, k, YS - k)) % YS

    def kv_to(n):
        to = nearest(n)
        for kind, ref in ((0, k_ref), (1, v_ref)):
            place = first + 2 * to + kind
            send(columns(ref, to, FEATURES), own_ref.at[first + p_me], s_kv, r_kv.at[y], s, place, place == u)

    loop(YS, kv_to)
    for z in range(2):
        place = z * HALF + u // 2
        for kind, stat, mem in ((0, lse_ref, mk_ref), (1, delta_ref, mv_ref)):
            send(stat.at[z], stat_ref.at[u % 2, kind], s_stat.at[z, kind], r_stat, s, place, place == u)
            send(mem, mem_ref.at[u % 2, kind], s_mem.at[z, kind], r_mem, s, place, place == u)

    def q_to(n):
        p = 2 * nearest(n // 2) + n % 2
        here = p == p_me
        send(columns(q_ref, p, 2 * FEATURES), qh_ref.at[p_me], s_q, r_q.at[p_me], s, first + p, here)
        send(columns(do_ref, p, 2 * FEATURES), doh_ref.at[p_me], s_do, r_do.at[p_me], s, first + p, here)

    loop(HALF, q_to)
    near_ref[...] = jnp.zeros_like(near_ref)
    macc_ref[...] = jnp.zeros_like(macc_ref)
    for kind in range(2):
        terms_ref[kind, ZERO] = jnp.zeros((BLOCK, FEATURES), BF16)
    got_ref[ZERO] = jnp.zeros((BLOCK, FEATURES), BF16)
    chain_ref[LINKS] = jnp.zeros((BLOCK, FEATURES), F32)

    def kv_on(n):
        at = pl.ds(first + 2 * nearest(n), 2)
        piece = own_ref.at[at]
        wait(piece, r_kv.at[nearest(n)])
        remote(piece, piece, s_z, r_z, s, (u + HALF) % PLACES).start()
        remote(piece, pool_ref.at[core, at], s_core.at[0], r_core.at[0], s, core_peer).start()
        pltpu.make_async_copy(piece, pool_ref.at[core, at], c_own.at[0]).start()

    loop(YS, kv_on)
    mine, theirs = pl.ds(first, HALF), pl.ds(second, HALF)
    wait(pool_ref.at[core, mine], c_own.at[0])
    wait(pool_ref.at[1 - core, mine], r_core.at[0])
    wait(stat_ref, r_stat)
    wait(mem_ref, r_mem)

    def dot(a, b, i, j):
        return lax.dot_general(a, b, (((i,), (j,)), ((), ())), preferred_element_type=F32)

    def block(j):
        q = [qh_ref[j, :, FEATURES * i : FEATURES * (i + 1)] for i in range(2)]
        do = [doh_ref[j, :, FEATURES * i : FEATURES * (i + 1)] for i in range(2)]
        lse, delta = [
            jnp.concatenate([stat_ref[i, kind, pl.ds(j, 1), :] for i in range(2)], axis=1) for kind in range(2)
        ]
        return q, do, lse, delta

    def pairs(keys, values, q2, do2, lse, delta, okay=None):
        weights = jnp.exp(dot(keys, q2, 1, 1) * SCALE - lse)
        dscores = weights * (dot(values, do2, 1, 1) - delta)
        if okay is not None:
            weights, dscores = jnp.where(okay, weights, 0.0), jnp.where(okay, dscores, 0.0)
        weight_bf, dscore_bf = weights.astype(BF16), dscores.astype(BF16)
        return dot(dscore_bf, q2, 1, 0) * SCALE, dot(weight_bf, do2, 1, 0), dot(dscore_bf, keys, 0, 0)

    def at_once(j):
        wait(qh_ref.at[j], r_q.at[j])
        wait(doh_ref.at[j], r_do.at[j])
        q, do, lse, delta = block(j)
        for i in range(2):
            cols = slice(FEATURES * i, FEATURES * (i + 1))
            dk, dv, dq = pairs(mem_ref[i, 0], mem_ref[i, 1], q[i], do[i], lse[:, cols], delta[:, cols])
            macc_ref[i, 0] += dk
            macc_ref[i, 1] += dv
            dq_ref[j, BLOCK * i : BLOCK * (i + 1)] = dq

        q2, do2 = jnp.concatenate(q, axis=0), jnp.concatenate(do, axis=0)

        def window(start, met, count):
            at, to = pl.ds(first + start, count), pl.ds(met, count)
            keys = pool_ref[0, at].reshape(count * BLOCK, FEATURES)
            values = pool_ref[1, at].reshape(count * BLOCK, FEATURES)
            dk, dv, dq = pairs(keys, values, q2, do2, lse, delta)
            near_ref[0, to] += dk.reshape(count, BLOCK, FEATURES)
            near_ref[1, to] += dv.reshape(count, BLOCK, FEATURES)
            dq_ref[j] += dq

        inside = (j > 0) & (j < HALF - 1)
        pl.when(inside)(lambda: window(j - 1, j, 3))
        pl.when(jnp.logical_not(inside))(lambda: window(jnp.where(j == 0, 0, HALF - 2), jnp.where(j == 0, 1, HALF - 1), 2))

    def in_order(n):
        at_once(2 * nearest(n // 2) + n % 2)

    loop(MIDDLE, in_order)
    wait(own_ref.at[theirs], r_z)
    onward = remote(own_ref.at[theirs], pool_ref.at[core, theirs], s_core.at[1], r_core.at[1], s, core_peer)
    onward.start()
    pltpu.make_async_copy(own_ref.at[theirs], pool_ref.at[core, theirs], c_own.at[1]).start()

    def far_to(t, place):
        out_ref[t] = own_ref[send_ref[t]]
        remote(out_ref.at[t], far_ref.at[s], s_far, r_far.at[s], t, place).start()

    far_peers(s, u, far_to)
    loop(LATE - MIDDLE, lambda n: in_order(n + MIDDLE))

    def far_on(t, place):
        wait(far_ref.at[t], r_far.at[t])
        at = pool_ref.at[core, PLACES + t]
        remote(far_ref.at[t], at, s_core.at[2], r_core.at[2], s, core_peer).start()
        pltpu.make_async_copy(far_ref.at[t], at, c_own.at[2]).start()

    far_peers(s, u, far_on)
    loop(HALF - LATE, lambda n: in_order(n + LATE))

    for i in range(2):
        for kind in range(2):
            for n in range(BLOCK // ROWS):
                dmem_ref[i * 4 + kind * 2 + n] = macc_ref[i, kind, ROWS * n : ROWS * (n + 1)]

    def part_to(r):
        remote(dmem_ref.at[r], parts_ref.at[r_me], s_part, r_part, part_peer(s, r), u).start()

    others(PARTS, r_me, part_to)
    rest = pl.ds(0, SPANS - 1)
    far_at = pl.ds(PLACES, SPANS - 1)
    wait(out_ref.at[rest], s_far)
    for n, at in ((1, theirs), (2, far_at)):
        wait(pool_ref.at[core, at], c_own.at[n])
        wait(pool_ref.at[1 - core, at], r_core.at[n])

    left_okay = (half > 0) | (s > 0)
    right_okay = (half == 0) | (s < SPANS - 1)
    left = jnp.where(half > 0, first - 1, jnp.where(s > 0, PLACES + s - 1, first))
    right = jnp.where(half == 0, HALF, jnp.where(s < SPANS - 1, PLACES + s + 1, first + HALF - 1))
    made = []
    for j, outer, okay in ((0, left, left_okay), (HALF - 1, right, right_okay)):
        q, do, lse, delta = block(j)
        q2, do2 = jnp.concatenate(q, axis=0), jnp.concatenate(do, axis=0)
        made.append(pairs(pool_ref[0, outer], pool_ref[1, outer], q2, do2, lse, delta, okay))
    for j, met, (dk, dv, dq) in ((0, 0, made[0]), (HALF - 1, NEAR - 1, made[1])):
        near_ref[0, met] += dk
        near_ref[1, met] += dv
        dq_ref[j] += dq

    def near_to(n):
        for kind in range(2):
            terms_ref[kind, ENTRIES + n] = near_ref[kind, n].astype(BF16)

    loop(NEAR, near_to)
    chunks = ENTRIES // CHUNK

    def terms_to(n, start, count):
        at = pl.ds(start, count)
        return remote(terms_ref.at[1 - core, at], got_ref.at[at], s_term.at[n], r_term.at[n], s, core_peer)

    terms_to(chunks, ENTRIES, NEAR).start()

    def random(n):
        made = []
        for j in (2 * n, 2 * n + 1):
            q, do, lse, delta = block(j)
            which = []
            for r in range(RANDOM):
                named = named_ref[j, r]
                which.append(jnp.where(named // PLACES == s, named % PLACES, PLACES + named // PLACES))
            keys = jnp.concatenate([pool_ref[0, w] for w in which], axis=0)
            values = jnp.concatenate([pool_ref[1, w] for w in which], axis=0)
            dk, dv, dq = pairs(
                keys, values, jnp.concatenate(q, axis=0), jnp.concatenate(do, axis=0), lse, delta
            )
            made.append((j, dk, dv, (dq_ref[j] + dq) * SCALE))
        for j, dk, dv, dq in made:
            at = pl.ds(RANDOM * j, RANDOM)
            terms_ref[0, at] = dk.astype(BF16).reshape(RANDOM, BLOCK, FEATURES)
            terms_ref[1, at] = dv.astype(BF16).reshape(RANDOM, BLOCK, FEATURES)
            for i in range(2):
                gq_ref[j, :, FEATURES * i : FEATURES * (i + 1)] = dq[BLOCK * i : BLOCK * (i + 1)].astype(BF16)
        for j, *_ in made:
            send(gq_ref.at[j], gq_out.at[p_me], s_gq, r_gq, s, first + j, j == p_me)
        per = CHUNK // RANDOM // 2

        @pl.when(n % per == per - 1)
        def _():
            terms_to(n // per, n // per * CHUNK, CHUNK).start()

    loop(HALF // 2, random)
    for n in range(chunks):
        terms_to(n, n * CHUNK, CHUNK).wait()
    terms_to(chunks, ENTRIES, NEAR).wait()

    def back_to(t, place):
        e = entry_ref[t]
        out_ref[t] = (terms_ref[core, e].astype(F32) + got_ref[e].astype(F32)).astype(BF16)
        remote(out_ref.at[t], back_ref.at[s], s_back, r_back.at[s], t, place).start()

    far_peers(s, u, back_to)

    wait(parts_ref.at[pl.ds(0, PARTS - 1)], r_part)
    parts_ref[r_me] = dmem_ref[r_me]
    part_ref[...] = jnp.sum(parts_ref[...], axis=0)

    def ring_to(r):
        remote(part_ref, rings_ref.at[ring_me], s_ring, r_ring, *ring_peer(r)).start()

    others(RINGS, ring_me, ring_to)

    def both(n):
        return terms_ref[core, n].astype(F32) + got_ref[n].astype(F32)

    def link(n):
        chain_ref[n] = both(n) + chain_ref[before_ref[n]]

    loop(ENTRIES, link)

    def link_back(t):
        wait(back_ref.at[t], r_back.at[t])
        chain_ref[ENTRIES + t] = back_ref[t].astype(F32) + chain_ref[before_ref[ENTRIES + t]]

    others(SPANS, s, link_back)
    each = HALF // CHUNKS
    swaps = []
    beside, edge = jnp.where(half == 0, 0, HALF - 1), jnp.where(half == 0, NEAR - 1, 0)

    def away(n):
        met = jnp.where(n == beside, both(ENTRIES + edge), 0.0)
        away_ref[n] = (chain_ref[last_ref[second + n]] + met).astype(BF16)

    for c in range(CHUNKS):
        loop(each, lambda i: away(c * each + i))
        at = pl.ds(c * each, each)
        swaps.append(remote(away_ref.at[at], came_ref.at[at], s_away.at[c], r_away.at[c], s, (u + HALF) % PLACES))
        swaps[-1].start()

    wait(rings_ref.at[pl.ds(0, RINGS - 1)], r_ring)
    rings_ref[ring_me] = part_ref[...]
    total_ref[...] = jnp.sum(rings_ref[...], axis=0)

    def mem_to(r):
        blk = part_peer(s, r)
        send(total_ref, mem_out.at[r_me % 4], s_out.at[r], r_out, blk, head, (blk == s) & (head == u))

    @pl.when(gives)
    def _():
        loop(PARTS, mem_to)

    for c in range(CHUNKS):
        swaps[c].wait_recv()

        def rows_to(i):
            p = c * each + i
            here = chain_ref[last_ref[first + p]] + both(ENTRIES + 1 + p)
            rows_out[p] = (here + came_ref[p].astype(F32)).astype(BF16)
            send(rows_out.at[p], rows_ref.at[p_me], s_rows, r_rows, s, first + p, p == p_me)

        loop(each, rows_to)
    wait(mem_out, r_out)
    wait(rows_ref, r_rows)
    wait(gq_out, r_gq)
    wait(rows_out.at[pl.ds(0, HALF - 1)], s_rows)
    wait(gq_ref.at[pl.ds(0, HALF - 1)], s_gq)
    wait(rings_ref.at[pl.ds(0, RINGS - 1)], s_ring)
    for c in range(CHUNKS):
        swaps[c].wait_send()

    @pl.when(gives)
    def _():
        takers(lambda r, blk: wait(total_ref, s_out.at[r]))

    wait(out_ref.at[rest], s_back)
    wait(parts_ref.at[pl.ds(0, PARTS - 1)], s_part)
    wait(own_ref.at[pl.ds(0, HALF - 1)], s_kv)
    wait(own_ref.at[mine], s_z)
    wait(own_ref.at[mine], s_core.at[0])
    onward.wait_send()
    wait(far_ref.at[rest], s_core.at[2])
    wait(qh_ref.at[pl.ds(0, HALF - 1)], s_q)
    wait(doh_ref.at[pl.ds(0, HALF - 1)], s_do)
    for z in range(2):
        @pl.when(z * HALF + u // 2 != u)
        def _():
            for kind in range(2):
                wait(stat_ref.at[0, kind], s_stat.at[z, kind])
                wait(mem_ref.at[0, kind], s_mem.at[z, kind])


def vmem(n):
    return [pl.BlockSpec(memory_space=pltpu.VMEM)] * n


def hbm(n):
    return [pl.BlockSpec(memory_space=pl.ANY)] * n


SMEM = pl.BlockSpec(memory_space=pltpu.SMEM)
DMA = pltpu.SemaphoreType.DMA


def shape(*dims, dtype=BF16):
    return jax.ShapeDtypeStruct(dims, dtype)


def attend_call(sends, entries, named, before, last, q, do, k, v, lse, delta, mk, mv):
    tile = (BLOCK, FEATURES)
    wide = (HALF, BLOCK, 2 * FEATURES)
    one, per_kind = DMA, DMA((2, 2))
    return pl.pallas_call(
        attend,
        in_specs=[SMEM] * 5 + hbm(8),
        out_specs=hbm(1) + vmem(2),
        out_shape=[shape(*wide), shape(HALF, *tile), shape(4, ROWS, FEATURES, dtype=F32)],
        scratch_shapes=[
            pltpu.VMEM(wide, BF16),
            pltpu.VMEM((LINKS + 1,) + tile, F32),
            pltpu.VMEM((SPANS,) + tile, BF16),
            pltpu.VMEM((ROWS, FEATURES), F32),
            pltpu.VMEM((HALF,) + tile, BF16),
            pltpu.VMEM((HALF,) + tile, BF16),
            pltpu.VMEM((HALF,) + tile, BF16),
            pltpu.VMEM((RINGS, ROWS, FEATURES), F32),
            pltpu.VMEM((ROWS, FEATURES), F32),
            pltpu.VMEM(wide, BF16),
            pltpu.VMEM(wide, BF16),
            pltpu.VMEM((PLACES,) + tile, BF16),
            pltpu.VMEM((SPANS,) + tile, BF16),
            pltpu.VMEM((SPANS,) + tile, BF16),
            pltpu.VMEM((2, PLACES + SPANS) + tile, BF16),
            pltpu.VMEM((2, ZERO + 1) + tile, BF16),
            pltpu.VMEM((ZERO + 1,) + tile, BF16),
            pltpu.VMEM((HALF, 2 * BLOCK, FEATURES), F32),
            pltpu.VMEM((2, NEAR) + tile, F32),
            pltpu.VMEM((2, 2) + tile, F32),
            pltpu.VMEM((2, 2, HALF, BLOCK), F32),
            pltpu.VMEM((2, 2) + tile, BF16),
            pltpu.VMEM((PARTS, ROWS, FEATURES), F32),
            pltpu.VMEM((PARTS, ROWS, FEATURES), F32),
            one, DMA((YS,)), one, DMA((HALF,)), one, DMA((HALF,)), one, one,
            DMA((3,)), DMA((3,)), DMA((3,)), one, DMA((SPANS,)), one, DMA((SPANS,)),
            per_kind, one, per_kind, one, DMA((5,)), DMA((5,)), one, one,
            one, one, DMA((CHUNKS,)), DMA((CHUNKS,)), one, one, one, one, DMA((PARTS,)), one,
        ],
        compiler_params=pltpu.CompilerParams(collective_id=0, has_side_effects=True),
        name="attend",
    )(sends, entries, named, before, last, q, do, k, v, lse, delta, mk, mv)


STEPS = 4


def finish(gq_ref, rows_ref, mem_ref, gq_out, dk_ref, dv_ref, mk_ref, mv_ref):
    for n in range(HALF // STEPS):
        gq_out[:, 2 * FEATURES * n : 2 * FEATURES * (n + 1)] = gq_ref[n]
    for n in range(KEY_HEADS // STEPS):
        cols = slice(FEATURES * n, FEATURES * (n + 1))
        dk_ref[:, cols] = rows_ref[2 * n].astype(F32)
        dv_ref[:, cols] = rows_ref[2 * n + 1].astype(F32)

    @pl.when(pl.program_id(0) == 0)
    def _():
        for n in range(2):
            mk_ref[ROWS * n : ROWS * (n + 1), :] = mem_ref[n]
            mv_ref[ROWS * n : ROWS * (n + 1), :] = mem_ref[2 + n]


def finish_call(gq, rows, mem):
    def part(dims):
        return pl.BlockSpec((dims[0] // STEPS,) + dims[1:], lambda i: (i, 0, 0))

    def columns(width):
        return pl.BlockSpec((BLOCK, width // STEPS), lambda i: (0, i))

    one = pl.BlockSpec((BLOCK, FEATURES), lambda i: (0, 0))
    wide, narrow = QUERY_HEADS * FEATURES, KEY_HEADS * FEATURES
    return pl.pallas_call(
        finish,
        grid=(STEPS,),
        in_specs=[part(gq.shape), part(rows.shape), pl.BlockSpec(mem.shape, lambda i: (0, 0, 0))],
        out_specs=[columns(wide), columns(narrow), columns(narrow), one, one],
        out_shape=[shape(BLOCK, wide)]
        + [shape(BLOCK, narrow, dtype=F32)] * 2
        + [shape(BLOCK, FEATURES, dtype=F32)] * 2,
        name="finish",
    )(gq, rows, mem)


def shards(queries, keys, values, grad_out, row_lse, row_delta, pattern, memory_keys, memory_values):
    span, place = lax.axis_index("blk"), lax.axis_index("uly")
    half = place // HALF
    flat = pattern.reshape(SPANS, PLACES * RANDOM)
    ids = jnp.arange(SPANS, dtype=jnp.int32)
    from_me = (flat // PLACES == span) & (ids != span)[:, None]
    read = jnp.sum(jnp.where(from_me, flat % PLACES, 0), axis=1)
    sends = jnp.where(jnp.abs(ids - span) == 1, jnp.where(ids > span, PLACES - 1, 0), read)
    named = lax.dynamic_slice(pattern, (span * PLACES + half * HALF, 0), (HALF, RANDOM))
    number = jnp.arange(ENTRIES, dtype=jnp.int32).reshape(1, HALF, RANDOM)
    names = (named // PLACES)[None] == ids[:, None, None]
    entries = ZERO + jnp.sum(jnp.where(names, number - ZERO, 0), axis=(1, 2))
    entries = jnp.where((ids == span - 1) & (half == 0), ENTRIES, entries)
    entries = jnp.where((ids == span + 1) & (half == 1), ENTRIES + NEAR - 1, entries)
    links = jnp.arange(LINKS, dtype=jnp.int32)
    blocks = jnp.concatenate(
        [jnp.where(named // PLACES == span, named % PLACES, -1).reshape(ENTRIES), jnp.where(ids == span, -1, sends)]
    )
    earlier = (blocks[:, None] == blocks[None]) & (links[:, None] > links[None])
    before = jnp.max(jnp.where(earlier, links[None], -1), axis=1)
    before = jnp.where(before < 0, LINKS, before)
    naming = blocks[None] == jnp.arange(PLACES, dtype=jnp.int32)[:, None]
    last = jnp.max(jnp.where(naming, links[None], -1), axis=1)
    last = jnp.where(last < 0, LINKS, last)

    rows = (2, HALF, BLOCK)
    return tuple(finish_call(*attend_call(
        sends, entries, named, before, last, queries, grad_out, keys, values,
        row_lse.reshape(rows), row_delta.reshape(rows), memory_keys, memory_values,
    )))


def solution(mesh):
    tokens = P(("blk", "uly"), None)
    heads = P(None, "uly")
    return jax.shard_map(
        shards,
        mesh=mesh,
        in_specs=(tokens, tokens, tokens, tokens, P("blk", "uly"), P("blk", "uly"), P(), heads, heads),
        out_specs=(tokens, tokens, tokens, heads, heads),
        check_vma=False,
    )
```

```python
import functools

import jax
import jax.numpy as jnp
from jax import lax
from jax.experimental import pallas as pl
from jax.experimental.pallas import tpu as pltpu
from jax.sharding import PartitionSpec as P

QUERY_HEADS = 32
KEY_HEADS = 8
FEATURES = 128
BLOCK = 128
RANDOM = 2
SLOTS = 3 + RANDOM
SCALE = FEATURES ** (-0.5)
MESH = pl.DeviceIdType.MESH

SPANS, PLACES = 24, 32
HALF = PLACES // 2
YS = HALF // 2
X, Z = 4, 6
PARTS = 8
ROWS = 4 * BLOCK // PARTS

F32, BF16 = jnp.float32, jnp.bfloat16


def position():
    s, u = lax.axis_index("blk"), lax.axis_index("uly")
    return s, u, u // HALF, u % HALF, u % 2


def far_peers(s, u, body):
    x, a = s % X, s // X
    half, p = u // HALF, u % HALF
    odd = x % 2

    def along(step):
        lo = a + step
        crossed = (lo < 0) | (lo >= Z)
        lo = jnp.where(lo < 0, lo + Z, jnp.where(lo >= Z, lo - Z, lo))
        return lo * X, jnp.where(crossed, 1 - half, half) * HALF + p

    for step in (0, 1, -1, 2, -2):
        base, place = along(step)
        for xx in range(X):
            if step:
                body(base + xx, place)
            else:
                pl.when(x != xx)(functools.partial(body, base + xx, place))
    base = jnp.where(a < Z // 2, a + Z // 2, a - Z // 2) * X
    within, across = half * HALF + p, (1 - half) * HALF + p
    even_place = jnp.where(odd == 0, within, across)
    odd_place = jnp.where(odd == 0, across, within)
    for xx in range(X):
        body(base + xx, odd_place if xx % 2 else even_place)


def remote(src, dst, sent, got, blk, uly):
    return pltpu.make_async_remote_copy(
        src_ref=src, dst_ref=dst, send_sem=sent, recv_sem=got, device_id=(blk, uly), device_id_type=MESH
    )


def send(src, dst, sent, got, blk, uly, here):
    @pl.when(jnp.logical_not(here))
    def _():
        remote(src, dst, sent, got, blk, uly).start()

    @pl.when(here)
    def _():
        pltpu.make_async_copy(src, dst, got).start()


def wait(ref, sem):
    pltpu.make_async_copy(ref, ref, sem).wait()


def loop(n, body):
    def step(i, carry):
        body(i)
        return carry

    lax.fori_loop(0, n, step, 0)


def greet(blk, uly):
    pl.semaphore_signal(pltpu.get_barrier_semaphore(), inc=1, device_id=(blk, uly), device_id_type=MESH)


def others(n, me, body):
    def step(i):
        @pl.when(i != me)
        def _():
            body(i)

    loop(n, step)


def part_peer(s, r):
    return ((s // X) // 2 * 2 + r % 2) * X + r // 2


def my_part(s):
    return s % X * 2 + s // X % 2


ENTRIES = HALF * RANDOM
NEAR = HALF + 2
ZERO = ENTRIES + NEAR
LINKS = ENTRIES + SPANS
CHUNKS = 4
RINGS = 6
CHUNK = 8
MIDDLE = 8
LATE = 14


def attend(
    send_ref, entry_ref, named_ref, before_ref, last_ref,
    q_ref, do_ref, k_ref, v_ref, lse_ref, delta_ref, mk_ref, mv_ref,
    gq_out, rows_ref, mem_out,
    gq_ref, chain_ref, back_ref, part_ref, away_ref, came_ref, rows_out, rings_ref, total_ref,
    qh_ref, doh_ref, own_ref, far_ref, out_ref, pool_ref, terms_ref, got_ref, dq_ref, near_ref, macc_ref,
    stat_ref, mem_ref, dmem_ref, parts_ref,
    s_kv, r_kv, s_q, r_q, s_do, r_do, s_z, r_z, s_core, r_core, c_own, s_far, r_far, s_back, r_back,
    s_stat, r_stat, s_mem, r_mem, s_term, r_term, s_part, r_part,
    s_gq, r_gq, s_away, r_away, s_rows, r_rows, s_ring, r_ring, s_out, r_out,
):
    s, u, half, p_me, core = position()
    y, first = p_me // 2, half * HALF
    second = HALF - first
    core_peer = u + 1 - 2 * core
    r_me = my_part(s)
    ring_me = (s // X) // 2 * 2 + half
    head = 4 * y + 2 * core + r_me // 4
    source = first + u // 2

    def ring_peer(r):
        return ((r // 2) * 2 + s // X % 2) * X + s % X, r % 2 * HALF + p_me

    gives = half == y // 4

    def takers(body):
        def step(r):
            blk = part_peer(s, r)

            @pl.when(jnp.logical_not((blk == s) & (head == u)))
            def _():
                body(r, blk)

        loop(PARTS, step)

    def givers(body):
        def step(n):
            blk = part_peer(s, u % 2 * 4 + n)

            @pl.when(jnp.logical_not((blk == s) & (source == u)))
            def _():
                body(blk)

        loop(4, step)

    others(PLACES, u, lambda p: greet(s, p))
    far_peers(s, u, greet)
    others(PARTS, r_me, lambda r: greet(part_peer(s, r), u))
    others(RINGS, ring_me, lambda r: greet(*ring_peer(r)))

    @pl.when(gives)
    def _():
        takers(lambda r, blk: greet(blk, head))

    givers(lambda blk: greet(blk, source))
    own = ((r_me // 4 == u % 2) & (source == u)).astype(jnp.int32)
    count = PLACES - 1 + SPANS - 1 + PARTS - 1 + RINGS - 1 + 4 - own + jnp.where(gives, PARTS - own, 0)
    pl.semaphore_wait(pltpu.get_barrier_semaphore(), count)

    def columns(ref, i, width):
        return ref.at[:, pl.ds(pl.multiple_of(i * width, width), width)]

    def nearest(n):
        k = (n + 1) // 2
        return (y + jnp.where(n % 2 == 1, k, YS - k)) % YS

    def kv_to(n):
        to = nearest(n)
        for kind, ref in ((0, k_ref), (1, v_ref)):
            place = first + 2 * to + kind
            send(columns(ref, to, FEATURES), own_ref.at[first + p_me], s_kv, r_kv.at[y], s, place, place == u)

    loop(YS, kv_to)
    for z in range(2):
        place = z * HALF + u // 2
        for kind, stat, mem in ((0, lse_ref, mk_ref), (1, delta_ref, mv_ref)):
            send(stat.at[z], stat_ref.at[u % 2, kind], s_stat.at[z, kind], r_stat, s, place, place == u)
            send(mem, mem_ref.at[u % 2, kind], s_mem.at[z, kind], r_mem, s, place, place == u)

    def q_to(n):
        p = 2 * nearest(n // 2) + n % 2
        here = p == p_me
        send(columns(q_ref, p, 2 * FEATURES), qh_ref.at[p_me], s_q, r_q.at[p_me], s, first + p, here)
        send(columns(do_ref, p, 2 * FEATURES), doh_ref.at[p_me], s_do, r_do.at[p_me], s, first + p, here)

    near_ref[...] = jnp.zeros_like(near_ref)
    macc_ref[...] = jnp.zeros_like(macc_ref)
    for kind in range(2):
        terms_ref[kind, ZERO] = jnp.zeros((BLOCK, FEATURES), BF16)
    got_ref[ZERO] = jnp.zeros((BLOCK, FEATURES), BF16)
    chain_ref[LINKS] = jnp.zeros((BLOCK, FEATURES), F32)

    def kv_on(n):
        at = pl.ds(first + 2 * nearest(n), 2)
        piece = own_ref.at[at]
        wait(piece, r_kv.at[nearest(n)])
        remote(piece, piece, s_z, r_z, s, (u + HALF) % PLACES).start()
        remote(piece, pool_ref.at[core, at], s_core.at[0], r_core.at[0], s, core_peer).start()
        pltpu.make_async_copy(piece, pool_ref.at[core, at], c_own.at[0]).start()
        q_to(2 * n)
        q_to(2 * n + 1)

    loop(YS, kv_on)
    mine, theirs = pl.ds(first, HALF), pl.ds(second, HALF)
    wait(pool_ref.at[core, mine], c_own.at[0])
    wait(pool_ref.at[1 - core, mine], r_core.at[0])
    wait(stat_ref, r_stat)
    wait(mem_ref, r_mem)

    def dot(a, b, i, j):
        return lax.dot_general(a, b, (((i,), (j,)), ((), ())), preferred_element_type=F32)

    def block(j):
        q = [qh_ref[j, :, FEATURES * i : FEATURES * (i + 1)] for i in range(2)]
        do = [doh_ref[j, :, FEATURES * i : FEATURES * (i + 1)] for i in range(2)]
        lse, delta = [
            jnp.concatenate([stat_ref[i, kind, pl.ds(j, 1), :] for i in range(2)], axis=1) for kind in range(2)
        ]
        return q, do, lse, delta

    def pairs(keys, values, q2, do2, lse, delta, okay=None):
        weights = jnp.exp(dot(keys, q2, 1, 1) * SCALE - lse)
        dscores = weights * (dot(values, do2, 1, 1) - delta)
        if okay is not None:
            weights, dscores = jnp.where(okay, weights, 0.0), jnp.where(okay, dscores, 0.0)
        weight_bf, dscore_bf = weights.astype(BF16), dscores.astype(BF16)
        return dot(dscore_bf, q2, 1, 0) * SCALE, dot(weight_bf, do2, 1, 0), dot(dscore_bf, keys, 0, 0)

    def at_once(j):
        wait(qh_ref.at[j], r_q.at[j])
        wait(doh_ref.at[j], r_do.at[j])
        q, do, lse, delta = block(j)
        for i in range(2):
            cols = slice(FEATURES * i, FEATURES * (i + 1))
            dk, dv, dq = pairs(mem_ref[i, 0], mem_ref[i, 1], q[i], do[i], lse[:, cols], delta[:, cols])
            macc_ref[i, 0] += dk
            macc_ref[i, 1] += dv
            dq_ref[j, BLOCK * i : BLOCK * (i + 1)] = dq

        q2, do2 = jnp.concatenate(q, axis=0), jnp.concatenate(do, axis=0)

        def window(start, met, count):
            at, to = pl.ds(first + start, count), pl.ds(met, count)
            keys = pool_ref[0, at].reshape(count * BLOCK, FEATURES)
            values = pool_ref[1, at].reshape(count * BLOCK, FEATURES)
            dk, dv, dq = pairs(keys, values, q2, do2, lse, delta)
            near_ref[0, to] += dk.reshape(count, BLOCK, FEATURES)
            near_ref[1, to] += dv.reshape(count, BLOCK, FEATURES)
            dq_ref[j] += dq

        inside = (j > 0) & (j < HALF - 1)
        pl.when(inside)(lambda: window(j - 1, j, 3))
        pl.when(jnp.logical_not(inside))(lambda: window(jnp.where(j == 0, 0, HALF - 2), jnp.where(j == 0, 1, HALF - 1), 2))

    def in_order(n):
        at_once(2 * nearest(n // 2) + n % 2)

    loop(MIDDLE, in_order)
    wait(own_ref.at[theirs], r_z)
    onward = remote(own_ref.at[theirs], pool_ref.at[core, theirs], s_core.at[1], r_core.at[1], s, core_peer)
    onward.start()
    pltpu.make_async_copy(own_ref.at[theirs], pool_ref.at[core, theirs], c_own.at[1]).start()

    def far_to(t, place):
        out_ref[t] = own_ref[send_ref[t]]
        remote(out_ref.at[t], far_ref.at[s], s_far, r_far.at[s], t, place).start()

    far_peers(s, u, far_to)
    loop(LATE - MIDDLE, lambda n: in_order(n + MIDDLE))

    def far_on(t, place):
        wait(far_ref.at[t], r_far.at[t])
        at = pool_ref.at[core, PLACES + t]
        remote(far_ref.at[t], at, s_core.at[2], r_core.at[2], s, core_peer).start()
        pltpu.make_async_copy(far_ref.at[t], at, c_own.at[2]).start()

    far_peers(s, u, far_on)
    loop(HALF - LATE, lambda n: in_order(n + LATE))

    for i in range(2):
        for kind in range(2):
            for n in range(BLOCK // ROWS):
                dmem_ref[i * 4 + kind * 2 + n] = macc_ref[i, kind, ROWS * n : ROWS * (n + 1)]

    def part_to(r):
        remote(dmem_ref.at[r], parts_ref.at[r_me], s_part, r_part, part_peer(s, r), u).start()

    others(PARTS, r_me, part_to)
    rest = pl.ds(0, SPANS - 1)
    far_at = pl.ds(PLACES, SPANS - 1)
    wait(out_ref.at[rest], s_far)
    for n, at in ((1, theirs), (2, far_at)):
        wait(pool_ref.at[core, at], c_own.at[n])
        wait(pool_ref.at[1 - core, at], r_core.at[n])

    left_okay = (half > 0) | (s > 0)
    right_okay = (half == 0) | (s < SPANS - 1)
    left = jnp.where(half > 0, first - 1, jnp.where(s > 0, PLACES + s - 1, first))
    right = jnp.where(half == 0, HALF, jnp.where(s < SPANS - 1, PLACES + s + 1, first + HALF - 1))
    made = []
    for j, outer, okay in ((0, left, left_okay), (HALF - 1, right, right_okay)):
        q, do, lse, delta = block(j)
        q2, do2 = jnp.concatenate(q, axis=0), jnp.concatenate(do, axis=0)
        made.append(pairs(pool_ref[0, outer], pool_ref[1, outer], q2, do2, lse, delta, okay))
    for j, met, (dk, dv, dq) in ((0, 0, made[0]), (HALF - 1, NEAR - 1, made[1])):
        near_ref[0, met] += dk
        near_ref[1, met] += dv
        dq_ref[j] += dq

    def near_to(n):
        for kind in range(2):
            terms_ref[kind, ENTRIES + n] = near_ref[kind, n].astype(BF16)

    loop(NEAR, near_to)
    chunks = ENTRIES // CHUNK

    def terms_to(n, start, count):
        at = pl.ds(start, count)
        return remote(terms_ref.at[1 - core, at], got_ref.at[at], s_term.at[n], r_term.at[n], s, core_peer)

    terms_to(chunks, ENTRIES, NEAR).start()

    def random(n):
        made = []
        for j in (2 * n, 2 * n + 1):
            q, do, lse, delta = block(j)
            which = []
            for r in range(RANDOM):
                named = named_ref[j, r]
                which.append(jnp.where(named // PLACES == s, named % PLACES, PLACES + named // PLACES))
            keys = jnp.concatenate([pool_ref[0, w] for w in which], axis=0)
            values = jnp.concatenate([pool_ref[1, w] for w in which], axis=0)
            dk, dv, dq = pairs(
                keys, values, jnp.concatenate(q, axis=0), jnp.concatenate(do, axis=0), lse, delta
            )
            made.append((j, dk, dv, (dq_ref[j] + dq) * SCALE))
        for j, dk, dv, dq in made:
            at = pl.ds(RANDOM * j, RANDOM)
            terms_ref[0, at] = dk.astype(BF16).reshape(RANDOM, BLOCK, FEATURES)
            terms_ref[1, at] = dv.astype(BF16).reshape(RANDOM, BLOCK, FEATURES)
            for i in range(2):
                gq_ref[j, :, FEATURES * i : FEATURES * (i + 1)] = dq[BLOCK * i : BLOCK * (i + 1)].astype(BF16)
        for j, *_ in made:
            send(gq_ref.at[j], gq_out.at[p_me], s_gq, r_gq, s, first + j, j == p_me)
        per = CHUNK // RANDOM // 2

        @pl.when(n % per == per - 1)
        def _():
            terms_to(n // per, n // per * CHUNK, CHUNK).start()

    loop(HALF // 4, random)
    wait(parts_ref.at[pl.ds(0, PARTS - 1)], r_part)
    parts_ref[r_me] = dmem_ref[r_me]
    part_ref[...] = jnp.sum(parts_ref[...], axis=0)

    def ring_to(r):
        remote(part_ref, rings_ref.at[ring_me], s_ring, r_ring, *ring_peer(r)).start()

    others(RINGS, ring_me, ring_to)
    loop(HALF // 4, lambda n: random(n + HALF // 4))
    for n in range(chunks):
        terms_to(n, n * CHUNK, CHUNK).wait()
    terms_to(chunks, ENTRIES, NEAR).wait()

    def back_to(t, place):
        e = entry_ref[t]
        out_ref[t] = (terms_ref[core, e].astype(F32) + got_ref[e].astype(F32)).astype(BF16)
        remote(out_ref.at[t], back_ref.at[s], s_back, r_back.at[s], t, place).start()

    far_peers(s, u, back_to)

    def both(n):
        return terms_ref[core, n].astype(F32) + got_ref[n].astype(F32)

    def link(n):
        chain_ref[n] = both(n) + chain_ref[before_ref[n]]

    loop(ENTRIES, link)
    wait(rings_ref.at[pl.ds(0, RINGS - 1)], r_ring)
    rings_ref[ring_me] = part_ref[...]
    total_ref[...] = jnp.sum(rings_ref[...], axis=0)

    def mem_to(r):
        blk = part_peer(s, r)
        send(total_ref, mem_out.at[r_me % 4], s_out.at[r], r_out, blk, head, (blk == s) & (head == u))

    @pl.when(gives)
    def _():
        loop(PARTS, mem_to)

    def link_back(t):
        wait(back_ref.at[t], r_back.at[t])
        chain_ref[ENTRIES + t] = back_ref[t].astype(F32) + chain_ref[before_ref[ENTRIES + t]]

    others(SPANS, s, link_back)
    each = HALF // CHUNKS
    swaps = []
    beside, edge = jnp.where(half == 0, 0, HALF - 1), jnp.where(half == 0, NEAR - 1, 0)

    def away(n):
        met = jnp.where(n == beside, both(ENTRIES + edge), 0.0)
        away_ref[n] = (chain_ref[last_ref[second + n]] + met).astype(BF16)

    for c in range(CHUNKS):
        loop(each, lambda i: away(c * each + i))
        at = pl.ds(c * each, each)
        swaps.append(remote(away_ref.at[at], came_ref.at[at], s_away.at[c], r_away.at[c], s, (u + HALF) % PLACES))
        swaps[-1].start()

    for c in range(CHUNKS):
        swaps[c].wait_recv()

        def rows_to(i):
            p = c * each + i
            here = chain_ref[last_ref[first + p]] + both(ENTRIES + 1 + p)
            rows_out[p] = (here + came_ref[p].astype(F32)).astype(BF16)
            send(rows_out.at[p], rows_ref.at[p_me], s_rows, r_rows, s, first + p, p == p_me)

        loop(each, rows_to)
    wait(mem_out, r_out)
    wait(rows_ref, r_rows)
    wait(gq_out, r_gq)
    wait(rows_out.at[pl.ds(0, HALF - 1)], s_rows)
    wait(gq_ref.at[pl.ds(0, HALF - 1)], s_gq)
    wait(rings_ref.at[pl.ds(0, RINGS - 1)], s_ring)
    for c in range(CHUNKS):
        swaps[c].wait_send()

    @pl.when(gives)
    def _():
        takers(lambda r, blk: wait(total_ref, s_out.at[r]))

    wait(out_ref.at[rest], s_back)
    wait(parts_ref.at[pl.ds(0, PARTS - 1)], s_part)
    wait(own_ref.at[pl.ds(0, HALF - 1)], s_kv)
    wait(own_ref.at[mine], s_z)
    wait(own_ref.at[mine], s_core.at[0])
    onward.wait_send()
    wait(far_ref.at[rest], s_core.at[2])
    wait(qh_ref.at[pl.ds(0, HALF - 1)], s_q)
    wait(doh_ref.at[pl.ds(0, HALF - 1)], s_do)
    for z in range(2):
        @pl.when(z * HALF + u // 2 != u)
        def _():
            for kind in range(2):
                wait(stat_ref.at[0, kind], s_stat.at[z, kind])
                wait(mem_ref.at[0, kind], s_mem.at[z, kind])


def vmem(n):
    return [pl.BlockSpec(memory_space=pltpu.VMEM)] * n


def hbm(n):
    return [pl.BlockSpec(memory_space=pl.ANY)] * n


SMEM = pl.BlockSpec(memory_space=pltpu.SMEM)
DMA = pltpu.SemaphoreType.DMA


def shape(*dims, dtype=BF16):
    return jax.ShapeDtypeStruct(dims, dtype)


def attend_call(sends, entries, named, before, last, q, do, k, v, lse, delta, mk, mv):
    tile = (BLOCK, FEATURES)
    wide = (HALF, BLOCK, 2 * FEATURES)
    one, per_kind = DMA, DMA((2, 2))
    return pl.pallas_call(
        attend,
        in_specs=[SMEM] * 5 + hbm(8),
        out_specs=hbm(1) + vmem(2),
        out_shape=[shape(*wide), shape(HALF, *tile), shape(4, ROWS, FEATURES, dtype=F32)],
        scratch_shapes=[
            pltpu.VMEM(wide, BF16),
            pltpu.VMEM((LINKS + 1,) + tile, F32),
            pltpu.VMEM((SPANS,) + tile, BF16),
            pltpu.VMEM((ROWS, FEATURES), F32),
            pltpu.VMEM((HALF,) + tile, BF16),
            pltpu.VMEM((HALF,) + tile, BF16),
            pltpu.VMEM((HALF,) + tile, BF16),
            pltpu.VMEM((RINGS, ROWS, FEATURES), F32),
            pltpu.VMEM((ROWS, FEATURES), F32),
            pltpu.VMEM(wide, BF16),
            pltpu.VMEM(wide, BF16),
            pltpu.VMEM((PLACES,) + tile, BF16),
            pltpu.VMEM((SPANS,) + tile, BF16),
            pltpu.VMEM((SPANS,) + tile, BF16),
            pltpu.VMEM((2, PLACES + SPANS) + tile, BF16),
            pltpu.VMEM((2, ZERO + 1) + tile, BF16),
            pltpu.VMEM((ZERO + 1,) + tile, BF16),
            pltpu.VMEM((HALF, 2 * BLOCK, FEATURES), F32),
            pltpu.VMEM((2, NEAR) + tile, F32),
            pltpu.VMEM((2, 2) + tile, F32),
            pltpu.VMEM((2, 2, HALF, BLOCK), F32),
            pltpu.VMEM((2, 2) + tile, BF16),
            pltpu.VMEM((PARTS, ROWS, FEATURES), F32),
            pltpu.VMEM((PARTS, ROWS, FEATURES), F32),
            one, DMA((YS,)), one, DMA((HALF,)), one, DMA((HALF,)), one, one,
            DMA((3,)), DMA((3,)), DMA((3,)), one, DMA((SPANS,)), one, DMA((SPANS,)),
            per_kind, one, per_kind, one, DMA((5,)), DMA((5,)), one, one,
            one, one, DMA((CHUNKS,)), DMA((CHUNKS,)), one, one, one, one, DMA((PARTS,)), one,
        ],
        compiler_params=pltpu.CompilerParams(collective_id=0, has_side_effects=True),
        name="attend",
    )(sends, entries, named, before, last, q, do, k, v, lse, delta, mk, mv)


STEPS = 4


def finish(gq_ref, rows_ref, mem_ref, gq_out, dk_ref, dv_ref, mk_ref, mv_ref):
    for n in range(HALF // STEPS):
        gq_out[:, 2 * FEATURES * n : 2 * FEATURES * (n + 1)] = gq_ref[n]
    for n in range(KEY_HEADS // STEPS):
        cols = slice(FEATURES * n, FEATURES * (n + 1))
        dk_ref[:, cols] = rows_ref[2 * n].astype(F32)
        dv_ref[:, cols] = rows_ref[2 * n + 1].astype(F32)

    @pl.when(pl.program_id(0) == 0)
    def _():
        for n in range(2):
            mk_ref[ROWS * n : ROWS * (n + 1), :] = mem_ref[n]
            mv_ref[ROWS * n : ROWS * (n + 1), :] = mem_ref[2 + n]


def finish_call(gq, rows, mem):
    def part(dims):
        return pl.BlockSpec((dims[0] // STEPS,) + dims[1:], lambda i: (i, 0, 0))

    def columns(width):
        return pl.BlockSpec((BLOCK, width // STEPS), lambda i: (0, i))

    one = pl.BlockSpec((BLOCK, FEATURES), lambda i: (0, 0))
    wide, narrow = QUERY_HEADS * FEATURES, KEY_HEADS * FEATURES
    return pl.pallas_call(
        finish,
        grid=(STEPS,),
        in_specs=[part(gq.shape), part(rows.shape), pl.BlockSpec(mem.shape, lambda i: (0, 0, 0))],
        out_specs=[columns(wide), columns(narrow), columns(narrow), one, one],
        out_shape=[shape(BLOCK, wide)]
        + [shape(BLOCK, narrow, dtype=F32)] * 2
        + [shape(BLOCK, FEATURES, dtype=F32)] * 2,
        name="finish",
    )(gq, rows, mem)


def shards(queries, keys, values, grad_out, row_lse, row_delta, pattern, memory_keys, memory_values):
    span, place = lax.axis_index("blk"), lax.axis_index("uly")
    half = place // HALF
    flat = pattern.reshape(SPANS, PLACES * RANDOM)
    ids = jnp.arange(SPANS, dtype=jnp.int32)
    from_me = (flat // PLACES == span) & (ids != span)[:, None]
    read = jnp.sum(jnp.where(from_me, flat % PLACES, 0), axis=1)
    sends = jnp.where(jnp.abs(ids - span) == 1, jnp.where(ids > span, PLACES - 1, 0), read)
    named = lax.dynamic_slice(pattern, (span * PLACES + half * HALF, 0), (HALF, RANDOM))
    number = jnp.arange(ENTRIES, dtype=jnp.int32).reshape(1, HALF, RANDOM)
    names = (named // PLACES)[None] == ids[:, None, None]
    entries = ZERO + jnp.sum(jnp.where(names, number - ZERO, 0), axis=(1, 2))
    entries = jnp.where((ids == span - 1) & (half == 0), ENTRIES, entries)
    entries = jnp.where((ids == span + 1) & (half == 1), ENTRIES + NEAR - 1, entries)
    links = jnp.arange(LINKS, dtype=jnp.int32)
    blocks = jnp.concatenate(
        [jnp.where(named // PLACES == span, named % PLACES, -1).reshape(ENTRIES), jnp.where(ids == span, -1, sends)]
    )
    earlier = (blocks[:, None] == blocks[None]) & (links[:, None] > links[None])
    before = jnp.max(jnp.where(earlier, links[None], -1), axis=1)
    before = jnp.where(before < 0, LINKS, before)
    naming = blocks[None] == jnp.arange(PLACES, dtype=jnp.int32)[:, None]
    last = jnp.max(jnp.where(naming, links[None], -1), axis=1)
    last = jnp.where(last < 0, LINKS, last)

    rows = (2, HALF, BLOCK)
    return tuple(finish_call(*attend_call(
        sends, entries, named, before, last, queries, grad_out, keys, values,
        row_lse.reshape(rows), row_delta.reshape(rows), memory_keys, memory_values,
    )))


def solution(mesh):
    tokens = P(("blk", "uly"), None)
    heads = P(None, "uly")
    return jax.shard_map(
        shards,
        mesh=mesh,
        in_specs=(tokens, tokens, tokens, tokens, P("blk", "uly"), P("blk", "uly"), P(), heads, heads),
        out_specs=(tokens, tokens, tokens, heads, heads),
        check_vma=False,
    )
```
